32 devices in a mesh: parts: 2 (over x), branch: 16 (over z, y, core).
Axes of the slice: x: 2, y: 2, z: 4, core: 2. Of those that a mesh axis runs over, the one named last changes fastest.
Arguments:
- queries: bfloat16 [16384, 640], P(('parts', 'branch')), parts along dimension 0, may hold values from -144 to 144
- branch_keys: bfloat16 [16384, 128], P(('parts', 'branch')), parts along dimension 0, may hold values from -6 to 6
- branch_values: bfloat16 [16384, 128], P(('parts', 'branch')), parts along dimension 0, may hold values from -6 to 6
- prefix_keys: bfloat16 [4096, 128], P(('parts', 'branch')), parts along dimension 0, may hold values from -6 to 6
- prefix_values: bfloat16 [4096, 128], P(('parts', 'branch')), parts along dimension 0, may hold values from -6 to 6
- cotangent: bfloat16 [16384, 640], P(('parts', 'branch')), parts along dimension 0, may hold values from -6 to 6
- branch_len: int32 [32], P(('parts', 'branch')), parts along dimension 0, may hold values from 128 to 512, as said below
Outputs:
- attended: bfloat16 [16384, 640], P(('parts', 'branch')), parts along dimension 0
- grad_queries: bfloat16 [16384, 640], P(('parts', 'branch')), parts along dimension 0
- grad_branch_keys: bfloat16 [16384, 128], P(('parts', 'branch')), parts along dimension 0
- grad_branch_values: bfloat16 [16384, 128], P(('parts', 'branch')), parts along dimension 0
- grad_prefix_keys: float32 [4096, 128], P(('parts', 'branch')), parts along dimension 0
- grad_prefix_values: float32 [4096, 128], P(('parts', 'branch')), parts along dimension 0
The draws below stay inside these ranges and needn't reach their ends.
There are 2 independent parts, one for each index of `parts`. The reference program is written for one: setup_inputs(seed, part) draws one part's arguments, and reference() takes and returns one part's arrays. A program takes and returns all parts, laid end to end along the dimension named above; each array names one. Nothing has to cross between parts.
Inputs may be any that keep to these rules, and one draw needn't show every extreme that they name: `branch_len`: branch b's live tokens fill its slots from slot 0; in every draw some branch has 512 live tokens and some other branch 512 // 4.
All inputs are finite; a program needn't handle non-finite values.
Results may differ from the reference program's by a relative error of at most 0.008.
Values may be sent and summed in bfloat16 or wider, within the bound.
No kernel may reach another device: no remote copies, remote signals or barrier semaphores. Data moves between devices by JAX's collectives and lax.ppermute only.
A program may use at most 64 MiB of HBM per device.

```python
import jax
import jax.numpy as jnp
from jax import lax

DH = 128
H = 5
P_SIZE = 2048
TOK_DEV = 512
ROWS = 8192
N_BRANCH = 16


def joint_draw(key):
    folded = jax.random.fold_in(key, 11)
    query_key, prefix_key = jax.random.split(folded, 2)
    prefix_rows = jnp.clip(jax.random.normal(prefix_key, (P_SIZE, DH), jnp.float32), -6.0, 6.0)
    query_rows = jnp.clip(jax.random.normal(query_key, (ROWS, H * DH), jnp.float32), -6.0, 6.0)
    return (query_rows, prefix_rows)


def draw_queries(key, part):
    return joint_draw(key)[0].astype(jnp.bfloat16)


def draw_prefix_keys(key, part):
    return joint_draw(key)[1].astype(jnp.bfloat16)


def draw_branch_len(key, part):
    folded = jax.random.fold_in(key, 5)
    len_key, shuffle_key = jax.random.split(folded)
    lengths = jax.random.randint(len_key, (N_BRANCH,), TOK_DEV // 4, TOK_DEV + 1)
    shuffled = jax.random.permutation(shuffle_key, N_BRANCH)
    lengths = lengths.at[shuffled[0]].set(TOK_DEV).at[shuffled[1]].set(TOK_DEV // 4)
    return lengths.astype(jnp.int32)


def levels(stream_key, dims, shards, low, high):
    level, own = 1.0, jax.random.fold_in(stream_key, 6)
    for axis_at, parts in shards:
        heights = jnp.exp(jax.random.uniform(jax.random.fold_in(own, axis_at), (parts,), jnp.float32, low / len(shards), high / len(shards)))
        level = level * jnp.repeat(heights, dims[axis_at] // parts).reshape([-1 if axis == axis_at else 1 for axis in range(len(dims))])
    return level


def noise(stream_key, extent, scale, reach, cuts=(), kind=jnp.bfloat16):
    values = scale * jax.random.normal(stream_key, extent, jnp.float32)
    if cuts:
        values = values * levels(stream_key, extent, cuts, -0.22, 0.18)
    return jnp.clip(values, -reach, reach).astype(kind)


def setup_inputs(seed: int = 0, part: int = 0) -> dict:
    key_list = jax.random.split(jax.random.key(seed), 8)
    own_keys = jax.random.split(jax.random.fold_in(key_list[7], part), 8)
    return {
        "queries": draw_queries(jax.random.fold_in(jax.random.fold_in(key_list[7], part), 71), part),
        "branch_keys": noise(own_keys[1], (ROWS, DH), 1.0, 6.0, ((0, 16),)),
        "branch_values": noise(own_keys[2], (ROWS, DH), 1.0, 6.0, ((0, 16),)),
        "prefix_keys": draw_prefix_keys(jax.random.fold_in(jax.random.fold_in(key_list[7], part), 71), part),
        "prefix_values": noise(own_keys[4], (P_SIZE, DH), 1.0, 6.0, ((0, 16),)),
        "cotangent": noise(own_keys[5], (ROWS, H * DH), 1.0, 6.0, ((0, 16),)),
        "branch_len": draw_branch_len(jax.random.fold_in(jax.random.fold_in(key_list[7], part), 71), part),
    }


def branch_pass(query_rows, key_rows, value_rows, grad_rows, length, prefix_keys, prefix_values):
    slot_count = query_rows.shape[0]
    factor = DH ** -0.5
    live_slots = jnp.arange(slot_count) < length
    masked = grad_rows * live_slots[:, None].astype(grad_rows.dtype)
    query_flat = query_rows.reshape(slot_count * H, DH)
    grad_flat = masked.reshape(slot_count * H, DH)
    row_slot = jnp.arange(slot_count * H) // H
    causal = jnp.arange(slot_count)[None, :] <= row_slot[:, None]
    pre_scores = jnp.dot(query_flat, prefix_keys.T, preferred_element_type=jnp.float32) * factor
    own_scores = jnp.where(causal, jnp.dot(query_flat, key_rows.T, preferred_element_type=jnp.float32) * factor, -jnp.inf)
    highest = jnp.maximum(pre_scores.max(axis=1), own_scores.max(axis=1))[:, None]
    pre_exp = jnp.exp(pre_scores - highest)
    own_exp = jnp.exp(own_scores - highest)
    denominator = pre_exp.sum(axis=1, keepdims=True) + own_exp.sum(axis=1, keepdims=True)
    pre_prob = pre_exp / denominator
    own_prob = own_exp / denominator
    pre_low = pre_prob.astype(jnp.bfloat16)
    own_low = own_prob.astype(jnp.bfloat16)
    row_live = (row_slot < length)[:, None]
    attended = jnp.dot(pre_low, prefix_values, preferred_element_type=jnp.float32) + jnp.dot(own_low, value_rows, preferred_element_type=jnp.float32)
    attended = jnp.where(row_live, attended, 0.0).astype(jnp.bfloat16).reshape(slot_count, H * DH)
    pre_dprob = jnp.dot(grad_flat, prefix_values.T, preferred_element_type=jnp.float32)
    own_dprob = jnp.dot(grad_flat, value_rows.T, preferred_element_type=jnp.float32)
    dot_sum = (pre_prob * pre_dprob).sum(axis=1, keepdims=True) + (own_prob * own_dprob).sum(axis=1, keepdims=True)
    pre_dscore = (pre_prob * (pre_dprob - dot_sum)).astype(jnp.bfloat16)
    own_dscore = (own_prob * (own_dprob - dot_sum)).astype(jnp.bfloat16)
    grad_query = (jnp.dot(pre_dscore, prefix_keys, preferred_element_type=jnp.float32) + jnp.dot(own_dscore, key_rows, preferred_element_type=jnp.float32)) * factor
    grad_query = grad_query.astype(jnp.bfloat16).reshape(slot_count, H * DH)
    grad_key = (jnp.dot(own_dscore.T, query_flat, preferred_element_type=jnp.float32) * factor).astype(jnp.bfloat16)
    grad_value = jnp.dot(own_low.T, grad_flat, preferred_element_type=jnp.float32).astype(jnp.bfloat16)
    prefix_gk = jnp.dot(pre_dscore.T, query_flat, preferred_element_type=jnp.float32) * factor
    prefix_gv = jnp.dot(pre_low.T, grad_flat, preferred_element_type=jnp.float32)
    return attended, grad_query, grad_key, grad_value, prefix_gk, prefix_gv


def reference(queries, branch_keys, branch_values, prefix_keys, prefix_values, cotangent, branch_len):
    stacked = (queries.reshape(N_BRANCH, TOK_DEV, H * DH), branch_keys.reshape(N_BRANCH, TOK_DEV, DH),
               branch_values.reshape(N_BRANCH, TOK_DEV, DH), cotangent.reshape(N_BRANCH, TOK_DEV, H * DH),
               branch_len)

    def per_branch(sums_now, pieces):
        results = branch_pass(pieces[0], pieces[1], pieces[2], pieces[3], pieces[4], prefix_keys, prefix_values)
        return (sums_now[0] + results[4], sums_now[1] + results[5]), results[:4]

    zero_sums = (jnp.zeros((P_SIZE, DH), jnp.float32), jnp.zeros((P_SIZE, DH), jnp.float32))
    (prefix_gk, prefix_gv), results = lax.scan(per_branch, zero_sums, stacked)
    return (results[0].reshape(ROWS, H * DH), results[1].reshape(ROWS, H * DH),
            results[2].reshape(ROWS, DH), results[3].reshape(ROWS, DH), prefix_gk, prefix_gv)
```

```python
import functools
import math

import jax
import jax.numpy as jnp
from jax import lax
from jax.experimental import pallas as pl
from jax.experimental.pallas import tpu as pltpu
from jax.sharding import PartitionSpec as P

F32, BF = jnp.float32, jnp.bfloat16
DH=128
def nn(a,b): return lax.dot_general(a,b,(((1,),(0,)),((),())),preferred_element_type=F32)
def nt(a,b): return lax.dot_general(a,b,(((1,),(1,)),((),())),preferred_element_type=F32)

def kernel(len_ref, q_ref, g_ref, kp_ref, vp_ref, kpt_ref, vpt_ref, kb_ref, vb_ref, kbt_ref, vbt_ref,
           att_ref, gq_ref, gkb_ref, gvb_ref, dk_ref, dv_ref,
           s_ref, p_ref, ds_ref, dk_acc, dv_acc, dkb_acc, dvb_acc, *, chunk, own):
    h = pl.program_id(0)
    heads = pl.num_programs(0)
    slots = q_ref.shape[0]
    prefix = kp_ref.shape[0]
    factor = DH ** -0.5
    scale = factor * math.log2(math.e)
    qt = q_ref[...].T
    gt = g_ref[...].T
    length = len_ref[0]
    live = lax.broadcasted_iota(jnp.int32, (1, slots), 1) < length
    own_blocks = [(u, u) for u in range(0, slots, own)]

    @pl.when(h == 0)
    def _():
        dk_acc[...] = jnp.zeros_like(dk_acc)
        dv_acc[...] = jnp.zeros_like(dv_acc)
        dkb_acc[...] = jnp.zeros_like(dkb_acc)
        dvb_acc[...] = jnp.zeros_like(dvb_acc)

    top = jnp.full((8, slots), -jnp.inf, F32)
    for u, t in own_blocks:
        s = nn(kb_ref[u:u+own, :], qt[:, t:])
        ok = (lax.broadcasted_iota(jnp.int32, s.shape, 0) + u) <= (lax.broadcasted_iota(jnp.int32, s.shape, 1) + t)
        s = jnp.where(ok, s, -jnp.inf)
        s_ref[prefix+u:prefix+u+own, t:] = s
        m = s.reshape(own//8, 8, slots-t).max(0)
        top = jnp.concatenate([top[:, :t], jnp.maximum(top[:, t:], m)], 1) if t else jnp.maximum(top, m)

    def score(i, top):
        r = pl.ds(pl.multiple_of(i*chunk, chunk), chunk)
        s = nn(kp_ref[r, :], qt)
        s_ref[r, :] = s
        return jnp.maximum(top, s.reshape(chunk//8, 8, slots).max(0))
    top = lax.fori_loop(0, prefix//chunk, score, top)
    m = top.max(0, keepdims=True) * scale

    def prob(i, tot):
        r = pl.ds(pl.multiple_of(i*chunk, chunk), chunk)
        p = jnp.exp2(s_ref[r, :]*scale - m)
        p_ref[r, :] = p.astype(BF)
        return tot + p.reshape(chunk//8, 8, slots).sum(0)
    tot = lax.fori_loop(0, prefix//chunk, prob, jnp.zeros((8, slots), F32))
    for u, t in own_blocks:
        p = jnp.exp2(s_ref[prefix+u:prefix+u+own, t:]*scale - m[:, t:])
        p_ref[prefix+u:prefix+u+own, t:] = p.astype(BF)
        if t: p_ref[prefix+u:prefix+u+own, :t] = jnp.zeros((own, t), BF)
        ps = p.reshape(own//8, 8, slots-t).sum(0)
        tot = jnp.concatenate([tot[:, :t], tot[:, t:] + ps], 1) if t else tot + ps
    inv = 1.0 / tot.sum(0, keepdims=True)
    ot = nn(vpt_ref[...], p_ref[:prefix, :]) + nn(vbt_ref[...], p_ref[prefix:, :])
    ot = jnp.where(live, ot * inv, 0.0)
    att_ref[...] = ot.T.astype(BF)
    gs = jnp.where(live, gt.astype(F32) * inv, 0.0).astype(BF)
    dot = (gs.astype(F32) * ot).sum(0, keepdims=True)

    def grad(i, c):
        r = pl.ds(pl.multiple_of(i*chunk, chunk), chunk)
        p = p_ref[r, :]
        ds = p * (nn(vp_ref[r, :], gs) - dot).astype(BF)
        ds_ref[r, :] = ds
        dv_acc[r, :] += nt(p, gs)
        dk_acc[r, :] += nt(ds, qt)
        return c
    lax.fori_loop(0, prefix//chunk, grad, 0)
    for u, t in own_blocks:
        p = p_ref[prefix+u:prefix+u+own, t:]
        ds = p * (nn(vb_ref[u:u+own, :], gs[:, t:]) - dot[:, t:]).astype(BF)
        ds_ref[prefix+u:prefix+u+own, t:] = ds
        if t: ds_ref[prefix+u:prefix+u+own, :t] = jnp.zeros((own, t), BF)
        dvb_acc[u:u+own, :] += nt(p, gs[:, t:])
        dkb_acc[u:u+own, :] += nt(ds, qt[:, t:])
    dqt = nn(kpt_ref[...], ds_ref[:prefix, :]) + nn(kbt_ref[...], ds_ref[prefix:, :])
    gq_ref[...] = (dqt * factor).T.astype(BF)

    @pl.when(h == heads - 1)
    def _():
        gkb_ref[...] = (dkb_acc[...] * factor).astype(BF)
        gvb_ref[...] = dvb_acc[...].astype(BF)
        dk_ref[...] = (dk_acc[...] * factor).astype(dk_ref.dtype)
        dv_ref[...] = dv_acc[...].astype(dv_ref.dtype)

def attend(length, q, g, kp, vp, kb, vb, *, chunk=256, own=256, out=BF):
    slots, width = q.shape
    heads = width // DH
    prefix = kp.shape[0]
    full = lambda a: pl.BlockSpec(a.shape, lambda h: (0,)*len(a.shape))
    head = pl.BlockSpec((slots, DH), lambda h: (0, h))
    args = (kp, vp, kp.T, vp.T, kb, vb, kb.T, vb.T)
    row = pl.BlockSpec((slots, DH), lambda h: (0, 0))
    pre = pl.BlockSpec((prefix, DH), lambda h: (0, 0))
    sds = jax.ShapeDtypeStruct
    return pl.pallas_call(
        functools.partial(kernel, chunk=chunk, own=own),
        grid=(heads,),
        in_specs=[pl.BlockSpec(memory_space=pltpu.SMEM), head, head] + [full(a) for a in args],
        out_specs=[head, head, row, row, pre, pre],
        out_shape=[sds((slots, width), BF), sds((slots, width), BF), sds((slots, DH), BF), sds((slots, DH), BF),
                   sds((prefix, DH), out), sds((prefix, DH), out)],
        scratch_shapes=[pltpu.VMEM((prefix+slots, slots), F32), pltpu.VMEM((prefix+slots, slots), BF),
                        pltpu.VMEM((prefix+slots, slots), BF),
                        pltpu.VMEM((prefix, DH), F32), pltpu.VMEM((prefix, DH), F32),
                        pltpu.VMEM((slots, DH), F32), pltpu.VMEM((slots, DH), F32)],
        name="attend",
    )(length, q, g, *args)


def stages(n):
    out, rest = [], n
    while rest > 2:
        if rest >= 8:
            step = rest // 4
            out.append((step, 2 * step, 3 * step))
            rest = step
        else:
            step = rest // 2
            out.append((step,))
            rest = step
    if rest == 2:
        out.append((1,))
    return out


def swap(x, offset, n):
    return lax.ppermute(x, "branch", [(i, i ^ offset) for i in range(n)])


def gather(x, n):
    for offsets in stages(n):
        x = jnp.concatenate([x] + [swap(x, o, n) for o in offsets], axis=0)
    return x


def scatter(x, n):
    for offsets in reversed(stages(n)):
        rows = x.shape[0] // (len(offsets) + 1)
        parts = [swap(x[rows * (i + 1): rows * (i + 2)].astype(BF), o, n) for i, o in enumerate(offsets)]
        x = x[:rows].astype(F32)
        for part in parts:
            x = x + part.astype(F32)
    return x


def on_device(queries, branch_keys, branch_values, prefix_keys, prefix_values, cotangent, branch_len):
    n = lax.axis_size("branch")
    both = gather(jnp.concatenate([prefix_keys, prefix_values], axis=1), n)
    att, gq, gkb, gvb, dk, dv = attend(
        branch_len, queries, cotangent, both[:, :DH], both[:, DH:], branch_keys, branch_values)
    total = scatter(jnp.concatenate([dk, dv], axis=1), n)
    return att, gq, gkb, gvb, total[:, :DH], total[:, DH:]


def solution(mesh):
    row = P(("parts", "branch"), None)
    return jax.shard_map(
        on_device, mesh=mesh, in_specs=(row,) * 6 + (P(("parts", "branch")),), out_specs=(row,) * 6, check_vma=False)
```

```python
import functools
import math

import jax
import jax.numpy as jnp
from jax import lax
from jax.experimental import pallas as pl
from jax.experimental.pallas import tpu as pltpu
from jax.sharding import PartitionSpec as P

DH = 128
FACTOR = DH ** -0.5
SCALE = FACTOR * math.log2(math.e)
F32, BF = jnp.float32, jnp.bfloat16
sds = jax.ShapeDtypeStruct
OWN = 256


def nn(a, b):
    return lax.dot_general(a, b, (((1,), (0,)), ((), ())), preferred_element_type=F32)


def nt(a, b):
    return lax.dot_general(a, b, (((1,), (1,)), ((), ())), preferred_element_type=F32)


def fold(x, op):
    return op(x.reshape(x.shape[0] // 8, 8, x.shape[1]), axis=0)


def own_forward(q_ref, kb_ref, vb_ref, p_ref, o_ref, m_ref, l_ref, vbt_ref, *, own):
    slots = q_ref.shape[0]

    @pl.when(pl.program_id(0) == 0)
    def _():
        vbt_ref[...] = vb_ref[...].T

    qt = q_ref[...].T
    blocks = range(0, slots, own)
    scores, top = [], None
    for u in blocks:
        s = nn(kb_ref[u:u + own, :], qt[:, u:])
        ok = lax.broadcasted_iota(jnp.int32, s.shape, 0) <= lax.broadcasted_iota(jnp.int32, s.shape, 1)
        s = jnp.where(ok, s, -jnp.inf)
        scores.append(s)
        t = fold(s, jnp.max)
        top = t if u == 0 else jnp.concatenate([top[:, :u], jnp.maximum(top[:, u:], t)], 1)
    m = top.max(0, keepdims=True) * SCALE
    for u, s in zip(blocks, scores):
        p = jnp.exp2(s * SCALE - m[:, u:])
        t = fold(p, jnp.sum)
        low = p.astype(BF)
        p_ref[0, u:u + own, u:] = low
        o = nn(vbt_ref[:, u:u + own], low)
        if u == 0:
            tot, out = t, o
        else:
            p_ref[0, u:u + own, :u] = jnp.zeros((own, u), BF)
            tot = jnp.concatenate([tot[:, :u], tot[:, u:] + t], 1)
            out = jnp.concatenate([out[:, :u], out[:, u:] + o], 1)
    o_ref[0] = out
    m_ref[0] = jnp.broadcast_to(m, (8, slots))
    l_ref[0] = jnp.broadcast_to(tot.sum(0, keepdims=True), (8, slots))


def prefix_pass(len_ref, q_ref, g_ref, near_ref, far_ref, oo_ref, mo_ref, lo_ref,
                att_ref, ds_ref, go_ref, do_ref, dnear_ref, dfar_ref,
                s_ref, p_ref, top_ref, qt_ref, vpt_ref, acc_ref):
    k = pl.program_id(0)
    heads = pl.num_programs(0) - 1
    slots = q_ref.shape[0]
    rows = near_ref.shape[0]
    now, last = k % 2, (k + 1) % 2
    halves = ((0, near_ref), (1, far_ref))

    def score():
        qt = q_ref[...].T
        qt_ref[now] = qt
        top = None
        for i, ref in halves:
            s = nn(ref[:, :DH], qt)
            s_ref[now, i] = s
            t = fold(s, jnp.max)
            top = t if top is None else jnp.maximum(top, t)
        top_ref[now] = top

    def finish():
        m = jnp.maximum(top_ref[last].max(0, keepdims=True) * SCALE, mo_ref[0, :1])
        alpha = jnp.exp2(mo_ref[0, :1] - m)
        tot = alpha * lo_ref[0, :1]
        ot = alpha * oo_ref[0]
        for i, ref in halves:
            p = jnp.exp2(s_ref[last, i] * SCALE - m)
            low = p.astype(BF)
            p_ref[i] = low
            ot = ot + nn(vpt_ref[i], low)
            tot = tot + fold(p, jnp.sum).sum(0, keepdims=True)
        live = lax.broadcasted_iota(jnp.int32, (1, slots), 1) < len_ref[0]
        inv = jnp.where(live, 1.0 / tot, 0.0)
        ot = ot * inv
        att_ref[...] = ot.T.astype(BF)
        gt = g_ref[...].T.astype(F32)
        gs = (gt * inv).astype(BF)
        go = (gt * (inv * alpha)).astype(BF)
        go_ref[0] = go
        do_ref[0] = jnp.broadcast_to((go.astype(F32) * ot).sum(0, keepdims=True), (8, slots))
        dot = (gs.astype(F32) * ot).sum(0, keepdims=True)
        qt = qt_ref[last]
        for i, ref in halves:
            p = p_ref[i]
            ds = p * (nn(ref[:, DH:], gs) - dot).astype(BF)
            ds_ref[0, i * rows:(i + 1) * rows, :] = ds
            acc_ref[i, 1] += nt(p, gs)
            acc_ref[i, 0] += nt(ds, qt)

    @pl.when(k == 0)
    def _():
        acc_ref[...] = jnp.zeros_like(acc_ref)
        for i, ref in halves:
            vpt_ref[i] = ref[:, DH:].T
        score()

    @pl.when((k > 0) & (k < heads))
    def _():
        finish()
        score()

    @pl.when(k == heads)
    def _():
        finish()
        for i, ref in ((0, dnear_ref), (1, dfar_ref)):
            ref[:, :DH] = (acc_ref[i, 0] * FACTOR).astype(BF)
            ref[:, DH:] = acc_ref[i, 1].astype(BF)


def own_backward(q_ref, near_ref, far_ref, kb_ref, vb_ref, ds_ref, p_ref, go_ref, do_ref, dk_in, dv_in, *rest, own):
    gq_ref, dk_out, dv_out, kpt_ref, kbt_ref = rest[-5:]
    h = pl.program_id(0)
    slots = q_ref.shape[0]
    rows = near_ref.shape[0]

    @pl.when(h == 0)
    def _():
        kpt_ref[:, :rows] = near_ref[...].T
        kpt_ref[:, rows:] = far_ref[...].T
        kbt_ref[...] = kb_ref[...].T
        dk_out[...] = dk_in[...]
        dv_out[...] = dv_in[...]

    qt = q_ref[...].T
    go = go_ref[0]
    dot = do_ref[0, :1]
    dq = nn(kpt_ref[...], ds_ref[0])
    for u in range(0, slots, own):
        p = p_ref[0, u:u + own, u:]
        ds = p * (nn(vb_ref[u:u + own, :], go[:, u:]) - dot[:, u:]).astype(BF)
        dv_out[u:u + own, :] += nt(p, go[:, u:])
        dk_out[u:u + own, :] += nt(ds, qt[:, u:])
        o = nn(kbt_ref[:, u:u + own], ds)
        dq = dq + o if u == 0 else jnp.concatenate([dq[:, :u], dq[:, u:] + o], 1)
    gq_ref[...] = (dq * FACTOR).T.astype(BF)


def whole(a):
    return pl.BlockSpec(a.shape, lambda h: (0,) * len(a.shape))


def run_own_forward(q, kb, vb):
    slots, width = q.shape
    heads = width // DH
    block = lambda *shape: pl.BlockSpec((1,) + shape, lambda h: (h, 0, 0))
    return pl.pallas_call(
        functools.partial(own_forward, own=min(OWN, slots)), grid=(heads,), name="own_forward",
        in_specs=[pl.BlockSpec((slots, DH), lambda h: (0, h)), whole(kb), whole(vb)],
        out_specs=[block(slots, slots), block(DH, slots), block(8, slots), block(8, slots)],
        out_shape=[sds((heads, slots, slots), BF), sds((heads, DH, slots), F32),
                   sds((heads, 8, slots), F32), sds((heads, 8, slots), F32)],
        scratch_shapes=[pltpu.VMEM((DH, slots), BF)],
    )(q, kb, vb)


def run_prefix(length, q, g, near, far, oo, mo, lo):
    slots, width = q.shape
    heads = width // DH
    rows = near.shape[0]
    back = lambda h: jnp.maximum(h - 1, 0)
    late = lambda *shape: pl.BlockSpec((1,) + shape, lambda h: (back(h), 0, 0))
    col = pl.BlockSpec((slots, DH), lambda h: (0, back(h)))
    return pl.pallas_call(
        prefix_pass, grid=(heads + 1,), name="prefix_pass",
        in_specs=[pl.BlockSpec(memory_space=pltpu.SMEM),
                  pl.BlockSpec((slots, DH), lambda h: (0, jnp.minimum(h, heads - 1))), col,
                  whole(near), whole(far), late(DH, slots), late(8, slots), late(8, slots)],
        out_specs=[col, late(2 * rows, slots), late(DH, slots), late(8, slots), whole(near), whole(near)],
        out_shape=[sds((slots, width), BF), sds((heads, 2 * rows, slots), BF), sds((heads, DH, slots), BF),
                   sds((heads, 8, slots), F32), sds(near.shape, BF), sds(near.shape, BF)],
        scratch_shapes=[pltpu.VMEM((2, 2, rows, slots), F32), pltpu.VMEM((2, rows, slots), BF),
                        pltpu.VMEM((2, 8, slots), F32), pltpu.VMEM((2, DH, slots), BF),
                        pltpu.VMEM((2, DH, rows), BF), pltpu.VMEM((2, 2, rows, DH), F32)],
    )(length, q, g, near, far, oo, mo, lo)


def run_own_backward(q, near, far, kb, vb, ds, po, go, do, dk, dv, gq, first, count):
    slots, width = q.shape
    rows = near.shape[0]
    held = () if gq is None else (gq,)
    col = pl.BlockSpec((slots, DH), lambda h: (0, h + first))
    block = lambda *shape: pl.BlockSpec((1,) + shape, lambda h: (h + first, 0, 0))
    keys = pl.BlockSpec((rows, DH), lambda h: (0, 0))
    return pl.pallas_call(
        functools.partial(own_backward, own=min(OWN, slots)), grid=(count,), name="own_backward",
        in_specs=[col, keys, keys, whole(kb), whole(vb), block(2 * rows, slots), block(slots, slots),
                  block(DH, slots), block(8, slots), whole(dk), whole(dv)] + [pl.BlockSpec(memory_space=pl.ANY)] * len(held),
        out_specs=[col, whole(dk), whole(dv)],
        out_shape=[sds((slots, width), BF), sds((slots, DH), F32), sds((slots, DH), F32)],
        scratch_shapes=[pltpu.VMEM((DH, 2 * rows), BF), pltpu.VMEM((DH, slots), BF)],
        input_output_aliases={11: 0} if held else {},
    )(q, near, far, kb, vb, ds, po, go, do, dk, dv, *held)


def stages(n):
    out, rest = [], n
    while rest > 2:
        step = rest // 4 if rest >= 8 else rest // 2
        out.append(tuple(range(step, rest, step)))
        rest = step
    return out


def swap(x, offset, n):
    return lax.ppermute(x, "branch", [(i, i ^ offset) for i in range(n)])


def on_device(queries, branch_keys, branch_values, prefix_keys, prefix_values, cotangent, branch_len):
    n = lax.axis_size("branch")
    slots, width = queries.shape
    heads = width // DH
    near = jnp.concatenate([prefix_keys, prefix_values], axis=1)
    own = run_own_forward(queries, branch_keys, branch_values)
    for at, offsets in enumerate(stages(n)):
        parts = [near] + [swap(near, o, n) for o in offsets]
        if at == 0:
            parts, own = lax.optimization_barrier((parts, own))
        near = jnp.concatenate(parts, axis=0)
    far = swap(near, 1, n)
    po, oo, mo, lo = own
    att, ds, go, do, dnear, dfar = run_prefix(branch_len, queries, cotangent, near, far, oo, mo, lo)

    total = dnear.astype(F32) + swap(dfar, 1, n).astype(F32)
    back = functools.partial(run_own_backward, queries, near, far, branch_keys, branch_values, ds, po, go, do)
    cuts = [heads * i // len(stages(n)) for i in range(len(stages(n)) + 1)]
    dk = dv = jnp.zeros((slots, DH), F32)
    gq = None
    for at, offsets in enumerate(reversed(stages(n))):
        rows = total.shape[0] // (len(offsets) + 1)
        parts = [swap(total[rows * (i + 1):rows * (i + 2)].astype(BF), o, n) for i, o in enumerate(offsets)]
        total = total[:rows]
        gq, dk, dv = back(dk, dv, gq, cuts[at], cuts[at + 1] - cuts[at])
        parts, gq, dk, dv = lax.optimization_barrier((parts, gq, dk, dv))
        for part in parts:
            total = total + part.astype(F32)
    return att, gq, (dk * FACTOR).astype(BF), dv.astype(BF), total[:, :DH], total[:, DH:]


def solution(mesh):
    row = P(("parts", "branch"), None)
    return jax.shard_map(
        on_device, mesh=mesh, in_specs=(row,) * 6 + (P(("parts", "branch")),), out_specs=(row,) * 6, check_vma=False)
```

```python
import functools
import math

import jax
import jax.numpy as jnp
from jax import lax
from jax.experimental import pallas as pl
from jax.experimental.pallas import tpu as pltpu
from jax.sharding import PartitionSpec as P

DH = 128
FACTOR = DH ** -0.5
SCALE = FACTOR * math.log2(math.e)
F32, BF = jnp.float32, jnp.bfloat16
sds = jax.ShapeDtypeStruct
OWN = 256


def nn(a, b):
    return lax.dot_general(a, b, (((1,), (0,)), ((), ())), preferred_element_type=F32)


def nt(a, b):
    return lax.dot_general(a, b, (((1,), (1,)), ((), ())), preferred_element_type=F32)


def fold(x, op):
    return op(x.reshape(x.shape[0] // 8, 8, x.shape[1]), axis=0)


def own_forward(q_ref, kb_ref, vb_ref, p_ref, o_ref, m_ref, l_ref, vbt_ref, *, own):
    slots = q_ref.shape[0]

    @pl.when(pl.program_id(0) == 0)
    def _():
        vbt_ref[...] = vb_ref[...].T

    qt = q_ref[...].T
    blocks = range(0, slots, own)
    scores, top = [], None
    for u in blocks:
        s = nn(kb_ref[u:u + own, :], qt[:, u:])
        ok = lax.broadcasted_iota(jnp.int32, s.shape, 0) <= lax.broadcasted_iota(jnp.int32, s.shape, 1)
        s = jnp.where(ok, s, -jnp.inf)
        scores.append(s)
        t = fold(s, jnp.max)
        top = t if u == 0 else jnp.concatenate([top[:, :u], jnp.maximum(top[:, u:], t)], 1)
    m = top.max(0, keepdims=True) * SCALE
    for u, s in zip(blocks, scores):
        p = jnp.exp2(s * SCALE - m[:, u:])
        t = fold(p, jnp.sum)
        low = p.astype(BF)
        p_ref[0, u:u + own, u:] = low
        o = nn(vbt_ref[:, u:u + own], low)
        if u == 0:
            tot, out = t, o
        else:
            p_ref[0, u:u + own, :u] = jnp.zeros((own, u), BF)
            tot = jnp.concatenate([tot[:, :u], tot[:, u:] + t], 1)
            out = jnp.concatenate([out[:, :u], out[:, u:] + o], 1)
    o_ref[0] = out
    m_ref[0] = jnp.broadcast_to(m, (8, slots))
    l_ref[0] = jnp.broadcast_to(tot.sum(0, keepdims=True), (8, slots))


def prefix_pass(len_ref, q_ref, g_ref, near_ref, far_ref, oo_ref, mo_ref, lo_ref,
                att_ref, ds_ref, go_ref, do_ref, dnear_ref, dfar_ref,
                s_ref, p_ref, top_ref, qt_ref, vpt_ref, acc_ref):
    k = pl.program_id(0)
    heads = pl.num_programs(0) - 1
    slots = q_ref.shape[0]
    rows = near_ref.shape[0]
    now, last = k % 2, (k + 1) % 2
    halves = ((0, near_ref), (1, far_ref))

    def score():
        qt = q_ref[...].T
        qt_ref[now] = qt
        top = None
        for i, ref in halves:
            s = nn(ref[:, :DH], qt)
            s_ref[now, i] = s
            t = fold(s, jnp.max)
            top = t if top is None else jnp.maximum(top, t)
        top_ref[now] = top

    def finish():
        m = jnp.maximum(top_ref[last].max(0, keepdims=True) * SCALE, mo_ref[0, :1])
        alpha = jnp.exp2(mo_ref[0, :1] - m)
        tot = alpha * lo_ref[0, :1]
        ot = alpha * oo_ref[0]
        for i, ref in halves:
            p = jnp.exp2(s_ref[last, i] * SCALE - m)
            low = p.astype(BF)
            p_ref[i] = low
            ot = ot + nn(vpt_ref[i], low)
            tot = tot + fold(p, jnp.sum).sum(0, keepdims=True)
        live = lax.broadcasted_iota(jnp.int32, (1, slots), 1) < len_ref[0]
        inv = jnp.where(live, 1.0 / tot, 0.0)
        ot = ot * inv
        att_ref[...] = ot.T.astype(BF)
        gt = g_ref[...].T.astype(F32)
        gs = (gt * inv).astype(BF)
        go = (gt * (inv * alpha)).astype(BF)
        go_ref[0] = go
        do_ref[0] = jnp.broadcast_to((go.astype(F32) * ot).sum(0, keepdims=True), (8, slots))
        dot = (gs.astype(F32) * ot).sum(0, keepdims=True)
        qt = qt_ref[last]
        for i, ref in halves:
            p = p_ref[i]
            ds = p * (nn(ref[:, DH:], gs) - dot).astype(BF)
            ds_ref[0, i * rows:(i + 1) * rows, :] = ds
            acc_ref[i, 1] += nt(p, gs)
            acc_ref[i, 0] += nt(ds, qt)

    @pl.when(k == 0)
    def _():
        acc_ref[...] = jnp.zeros_like(acc_ref)
        for i, ref in halves:
            vpt_ref[i] = ref[:, DH:].T
        score()

    @pl.when((k > 0) & (k < heads))
    def _():
        finish()
        score()

    @pl.when(k == heads)
    def _():
        finish()
        for i, ref in ((0, dnear_ref), (1, dfar_ref)):
            ref[:, :DH] = (acc_ref[i, 0] * FACTOR).astype(BF)
            ref[:, DH:] = acc_ref[i, 1].astype(BF)


def own_backward(q_ref, near_ref, far_ref, kb_ref, vb_ref, ds_ref, p_ref, go_ref, do_ref, *rest, own, first, last):
    gq_ref, dk_out, dv_out, kpt_ref, kbt_ref, dk_acc, dv_acc = rest[-7:]
    h = pl.program_id(0)
    slots = q_ref.shape[0]
    rows = near_ref.shape[0]

    @pl.when(h == 0)
    def _():
        kpt_ref[:, :rows] = near_ref[...].T
        kpt_ref[:, rows:] = far_ref[...].T
        kbt_ref[...] = kb_ref[...].T
        if first:
            dk_acc[...] = jnp.zeros_like(dk_acc)
            dv_acc[...] = jnp.zeros_like(dv_acc)
        else:
            dk_acc[...] = rest[0][...]
            dv_acc[...] = rest[1][...]

    qt = q_ref[...].T
    go = go_ref[0]
    dot = do_ref[0, :1]
    dq = nn(kpt_ref[...], ds_ref[0])
    for u in range(0, slots, own):
        p = p_ref[0, u:u + own, u:]
        ds = p * (nn(vb_ref[u:u + own, :], go[:, u:]) - dot[:, u:]).astype(BF)
        dv_acc[u:u + own, :] += nt(p, go[:, u:])
        dk_acc[u:u + own, :] += nt(ds, qt[:, u:])
        o = nn(kbt_ref[:, u:u + own], ds)
        dq = dq + o if u == 0 else jnp.concatenate([dq[:, :u], dq[:, u:] + o], 1)
    gq_ref[...] = (dq * FACTOR).T.astype(BF)

    @pl.when(h == pl.num_programs(0) - 1)
    def _():
        dk_out[...] = (dk_acc[...] * (FACTOR if last else 1.0)).astype(dk_out.dtype)
        dv_out[...] = dv_acc[...].astype(dv_out.dtype)


def room(mib):
    return pltpu.CompilerParams(vmem_limit_bytes=mib << 20)


def whole(a):
    return pl.BlockSpec(a.shape, lambda h: (0,) * len(a.shape))


def run_own_forward(q, kb, vb):
    slots, width = q.shape
    heads = width // DH
    block = lambda *shape: pl.BlockSpec((1,) + shape, lambda h: (h, 0, 0))
    return pl.pallas_call(
        functools.partial(own_forward, own=min(OWN, slots)), grid=(heads,), name="own_forward",
        in_specs=[pl.BlockSpec((slots, DH), lambda h: (0, h)), whole(kb), whole(vb)],
        out_specs=[block(slots, slots), block(DH, slots), block(8, slots), block(8, slots)],
        out_shape=[sds((heads, slots, slots), BF), sds((heads, DH, slots), F32),
                   sds((heads, 8, slots), F32), sds((heads, 8, slots), F32)],
        scratch_shapes=[pltpu.VMEM((DH, slots), BF)], compiler_params=room(10),
    )(q, kb, vb)


def run_prefix(length, q, g, near, far, oo, mo, lo):
    slots, width = q.shape
    heads = width // DH
    rows = near.shape[0]
    back = lambda h: jnp.maximum(h - 1, 0)
    late = lambda *shape: pl.BlockSpec((1,) + shape, lambda h: (back(h), 0, 0))
    col = pl.BlockSpec((slots, DH), lambda h: (0, back(h)))
    return pl.pallas_call(
        prefix_pass, grid=(heads + 1,), name="prefix_pass",
        in_specs=[pl.BlockSpec(memory_space=pltpu.SMEM),
                  pl.BlockSpec((slots, DH), lambda h: (0, jnp.minimum(h, heads - 1))), col,
                  whole(near), whole(far), late(DH, slots), late(8, slots), late(8, slots)],
        out_specs=[col, late(2 * rows, slots), late(DH, slots), late(8, slots), whole(near), whole(near)],
        out_shape=[sds((slots, width), BF), sds((heads, 2 * rows, slots), BF), sds((heads, DH, slots), BF),
                   sds((heads, 8, slots), F32), sds(near.shape, BF), sds(near.shape, BF)],
        scratch_shapes=[pltpu.VMEM((2, 2, rows, slots), F32), pltpu.VMEM((2, rows, slots), BF),
                        pltpu.VMEM((2, 8, slots), F32), pltpu.VMEM((2, DH, slots), BF),
                        pltpu.VMEM((2, DH, rows), BF), pltpu.VMEM((2, 2, rows, DH), F32)],
        compiler_params=room(36),
    )(length, q, g, near, far, oo, mo, lo)


def run_own_backward(q, near, far, kb, vb, ds, po, go, do, held, first, count):
    slots, width = q.shape
    rows = near.shape[0]
    args = (q, near, far, kb, vb, ds, po, go, do) + held[:2]
    last = first + count == width // DH
    row = pl.BlockSpec((slots, DH), lambda h: (0, 0))
    sums = sds((slots, DH), BF if last else F32)
    col = pl.BlockSpec((slots, DH), lambda h: (0, h + first))
    block = lambda *shape: pl.BlockSpec((1,) + shape, lambda h: (h + first, 0, 0))
    keys = pl.BlockSpec((rows, DH), lambda h: (0, 0))
    return pl.pallas_call(
        functools.partial(own_backward, own=min(OWN, slots), first=not held, last=last), grid=(count,), name="own_backward",
        in_specs=[col, keys, keys, whole(kb), whole(vb), block(2 * rows, slots), block(slots, slots),
                  block(DH, slots), block(8, slots)] + [row] * len(held[:2]) + [pl.BlockSpec(memory_space=pl.ANY)] * len(held[2:]),
        out_specs=[col, row, row],
        out_shape=[sds((slots, width), BF), sums, sums],
        scratch_shapes=[pltpu.VMEM((DH, 2 * rows), BF), pltpu.VMEM((DH, slots), BF),
                        pltpu.VMEM((slots, DH), F32), pltpu.VMEM((slots, DH), F32)],
        compiler_params=room(20),
        input_output_aliases={len(args): 0} if held else {},
    )(*args, *held[2:])


def stages(n):
    out, rest = [], n
    while rest > 2:
        step = rest // 4 if rest >= 8 else rest // 2
        out.append(tuple(range(step, rest, step)))
        rest = step
    return out


def swap(x, offset, n):
    return lax.ppermute(x, "branch", [(i, i ^ offset) for i in range(n)])


def on_device(queries, branch_keys, branch_values, prefix_keys, prefix_values, cotangent, branch_len):
    n = lax.axis_size("branch")
    slots, width = queries.shape
    heads = width // DH
    low = jnp.array(-jnp.inf, BF)
    near = jnp.maximum(lax.pad(prefix_keys, low, ((0, 0, 0), (0, DH, 0))), lax.pad(prefix_values, low, ((0, 0, 0), (DH, 0, 0))))
    own = run_own_forward(queries, branch_keys, branch_values)
    for at, offsets in enumerate(stages(n)):
        parts = [near] + [swap(near, o, n) for o in offsets]
        if at == 0:
            parts, own = lax.optimization_barrier((parts, own))
        near = jnp.concatenate(parts, axis=0)
    far = swap(near, 1, n)
    po, oo, mo, lo = own
    att, ds, go, do, dnear, dfar = run_prefix(branch_len, queries, cotangent, near, far, oo, mo, lo)

    total = dnear.astype(F32) + swap(dfar, 1, n).astype(F32)
    back = functools.partial(run_own_backward, queries, near, far, branch_keys, branch_values, ds, po, go, do)
    cuts = [heads * i // len(stages(n)) for i in range(len(stages(n)) + 1)]
    held = ()
    for at, offsets in enumerate(reversed(stages(n))):
        rows = total.shape[0] // (len(offsets) + 1)
        parts = [swap(total[rows * (i + 1):rows * (i + 2)].astype(BF), o, n) for i, o in enumerate(offsets)]
        total = total[:rows]
        gq, dk, dv = back(held, cuts[at], cuts[at + 1] - cuts[at])
        parts, held = lax.optimization_barrier((parts, (dk, dv, gq)))
        for part in parts:
            total = total + part.astype(F32)
    dk, dv, gq = held
    return att, gq, dk, dv, total[:, :DH], total[:, DH:]


def solution(mesh):
    row = P(("parts", "branch"), None)
    return jax.shard_map(
        on_device, mesh=mesh, in_specs=(row,) * 6 + (P(("parts", "branch")),), out_specs=(row,) * 6, check_vma=False)
```

```python
import functools
import math

import jax
import jax.numpy as jnp
from jax import lax
from jax.experimental import pallas as pl
from jax.experimental.pallas import tpu as pltpu
from jax.sharding import PartitionSpec as P

DH = 128
FACTOR = DH ** -0.5
SCALE = FACTOR * math.log2(math.e)
F32, BF = jnp.float32, jnp.bfloat16
sds = jax.ShapeDtypeStruct
VMEM = pl.BlockSpec(memory_space=pltpu.VMEM)
OWN = 256


def nn(a, b):
    return lax.dot_general(a, b, (((1,), (0,)), ((), ())), preferred_element_type=F32)


def nt(a, b):
    return lax.dot_general(a, b, (((1,), (1,)), ((), ())), preferred_element_type=F32)


def fold(x, op):
    return op(x.reshape(x.shape[0] // 8, 8, x.shape[1]), axis=0)


def steps(slots):
    own = min(OWN, slots)
    return [(u, u + own) for u in range(0, slots, own)]


def bring(q_any, g_any, kb_any, vb_any, qt_ref, gt_ref, kb_ref, vb_ref, kbt_ref, vbt_ref, q_ref, g_ref, sems):
    pairs = ((q_any, q_ref), (kb_any, kb_ref), (vb_any, vb_ref), (g_any, g_ref))
    copies = [pltpu.make_async_copy(a, b, sems.at[i]) for i, (a, b) in enumerate(pairs)]
    for c in copies:
        c.start()
    for c, a, b in ((copies[0], q_ref, qt_ref), (copies[1], kb_ref, kbt_ref),
                    (copies[2], vb_ref, vbt_ref), (copies[3], g_ref, gt_ref)):
        c.wait()
        if len(b.shape) == 2:
            b[...] = a[...].T
        else:
            for h in range(b.shape[0]):
                b[h] = a[:, h * DH:(h + 1) * DH].T


def first_forward(q_ref, kb_ref, vbt_ref, lo_ref, po_ref, pl_ref, o_ref, m_ref, l_ref, vlt_ref):
    h = pl.program_id(0)
    slots = q_ref.shape[2]

    @pl.when(h == 0)
    def _():
        vlt_ref[...] = lo_ref[:, DH:].T

    qt = q_ref[h]
    sl = nn(lo_ref[:, :DH], qt)
    top = fold(sl, jnp.max)
    scores = []
    for u, v in steps(slots):
        s = nn(kb_ref[u:v, :], qt[:, u:])
        ok = lax.broadcasted_iota(jnp.int32, s.shape, 0) <= lax.broadcasted_iota(jnp.int32, s.shape, 1)
        s = jnp.where(ok, s, -jnp.inf)
        scores.append(s)
        t = jnp.maximum(top[:, u:], fold(s, jnp.max))
        top = t if u == 0 else jnp.concatenate([top[:, :u], t], 1)
    m = top.max(0, keepdims=True) * SCALE
    p = jnp.exp2(sl * SCALE - m)
    low = p.astype(BF)
    pl_ref[h] = low
    tot = fold(p, jnp.sum)
    out = nn(vlt_ref[...], low)
    for (u, v), s in zip(steps(slots), scores):
        p = jnp.exp2(s * SCALE - m[:, u:])
        low = p.astype(BF)
        po_ref[h, u:v, u:] = low
        t = tot[:, u:] + fold(p, jnp.sum)
        o = out[:, u:] + nn(vbt_ref[:, u:v], low)
        tot = t if u == 0 else jnp.concatenate([tot[:, :u], t], 1)
        out = o if u == 0 else jnp.concatenate([out[:, :u], o], 1)
    o_ref[h] = out
    m_ref[h] = jnp.broadcast_to(m, (8, slots))
    l_ref[h] = jnp.broadcast_to(tot.sum(0, keepdims=True), (8, slots))


def rest_forward(len_ref, q_ref, g_ref, hi_ref, far_ref, o_ref, m_ref, l_ref,
                 att_ref, ph_ref, pf_ref, gs_ref, go_ref, dg_ref, do_ref,
                 sh_ref, sf_ref, top_ref, vht_ref, vft_ref):
    k = pl.program_id(0)
    heads = pl.num_programs(0) - 1
    slots = q_ref.shape[2]
    now, last = k % 2, (k + 1) % 2
    halves = ((hi_ref, sh_ref, ph_ref, vht_ref), (far_ref, sf_ref, pf_ref, vft_ref))

    def score():
        qt = q_ref[k]
        top = None
        for ref, s_ref, _, _ in halves:
            s = nn(ref[:, :DH], qt)
            s_ref[now] = s
            t = fold(s, jnp.max)
            top = t if top is None else jnp.maximum(top, t)
        top_ref[now] = top

    def finish():
        h = k - 1
        first = m_ref[h, :1]
        m = jnp.maximum(top_ref[last].max(0, keepdims=True) * SCALE, first)
        alpha = jnp.exp2(first - m)
        tot = alpha * l_ref[h, :1]
        ot = alpha * o_ref[h]
        for _, s_ref, p_ref, vt_ref in halves:
            p = jnp.exp2(s_ref[last] * SCALE - m)
            low = p.astype(BF)
            p_ref[h] = low
            ot = ot + nn(vt_ref[...], low)
            tot = tot + fold(p, jnp.sum).sum(0, keepdims=True)
        live = lax.broadcasted_iota(jnp.int32, (1, slots), 1) < len_ref[0]
        inv = jnp.where(live, 1.0 / tot, 0.0)
        ot = ot * inv
        att_ref[...] = ot.T.astype(BF)
        gt = g_ref[h].astype(F32)
        for scale, w_ref, d_ref in ((inv, gs_ref, dg_ref), (inv * alpha, go_ref, do_ref)):
            w = (gt * scale).astype(BF)
            w_ref[h] = w
            d_ref[h] = jnp.broadcast_to((w.astype(F32) * ot).sum(0, keepdims=True), (8, slots))

    @pl.when(k == 0)
    def _():
        vht_ref[...] = hi_ref[:, DH:].T
        vft_ref[...] = far_ref[:, DH:].T
        score()

    @pl.when((k > 0) & (k < heads))
    def _():
        finish()
        score()

    @pl.when(k == heads)
    def _():
        finish()


def gradients(p, kv, ws, dot):
    return p * (nn(kv, ws) - dot).astype(BF)


def rows_backward(q_ref, w_ref, d_ref, p_ref, kv_ref, dkv_ref, ds_ref, acc_ref):
    h = pl.program_id(0)

    @pl.when(h == 0)
    def _():
        acc_ref[...] = jnp.zeros_like(acc_ref)

    ws = w_ref[h]
    p = p_ref[h]
    ds = gradients(p, kv_ref[:, DH:], ws, d_ref[h, :1])
    ds_ref[h] = ds
    acc_ref[1] += nt(p, ws)
    acc_ref[0] += nt(ds, q_ref[h])

    @pl.when(h == pl.num_programs(0) - 1)
    def _():
        dkv_ref[:, :DH] = (acc_ref[0] * FACTOR).astype(BF)
        dkv_ref[:, DH:] = acc_ref[1].astype(BF)


def first_backward(q_ref, w_ref, d_ref, po_ref, pl_ref, kb_ref, vb_ref, lo_ref,
                   dkv_ref, dsl_ref, dso_ref, gk_ref, gv_ref, acc_ref, own_ref):
    h = pl.program_id(0)
    slots = q_ref.shape[2]

    @pl.when(h == 0)
    def _():
        acc_ref[...] = jnp.zeros_like(acc_ref)
        own_ref[...] = jnp.zeros_like(own_ref)

    ws, dot, qt = w_ref[h], d_ref[h, :1], q_ref[h]
    p = pl_ref[h]
    ds = gradients(p, lo_ref[:, DH:], ws, dot)
    dsl_ref[h] = ds
    acc_ref[1] += nt(p, ws)
    acc_ref[0] += nt(ds, qt)
    for u, v in steps(slots):
        p = po_ref[h, u:v, u:]
        ds = gradients(p, vb_ref[u:v, :], ws[:, u:], dot[:, u:])
        dso_ref[h, u:v, u:] = ds
        own_ref[1, u:v, :] += nt(p, ws[:, u:])
        own_ref[0, u:v, :] += nt(ds, qt[:, u:])

    @pl.when(h == pl.num_programs(0) - 1)
    def _():
        dkv_ref[:, :DH] = (acc_ref[0] * FACTOR).astype(BF)
        dkv_ref[:, DH:] = acc_ref[1].astype(BF)
        gk_ref[...] = (own_ref[0] * FACTOR).astype(BF)
        gv_ref[...] = own_ref[1].astype(BF)


def query_gradient(kbt_ref, lo_ref, hi_ref, far_ref, dso_ref, dsl_ref, dsh_ref, dsf_ref,
                   gq_ref, klt_ref, kht_ref, kft_ref):
    h = pl.program_id(0)
    slots = gq_ref.shape[0]

    @pl.when(h == 0)
    def _():
        klt_ref[...] = lo_ref[:, :DH].T
        kht_ref[...] = hi_ref[:, :DH].T
        kft_ref[...] = far_ref[:, :DH].T

    dq = nn(klt_ref[...], dsl_ref[h]) + nn(kht_ref[...], dsh_ref[h]) + nn(kft_ref[...], dsf_ref[h])
    for u, v in steps(slots):
        o = dq[:, u:] + nn(kbt_ref[:, u:v], dso_ref[h, u:v, u:])
        dq = o if u == 0 else jnp.concatenate([dq[:, :u], o], 1)
    gq_ref[...] = (dq * FACTOR).T.astype(BF)


def call(body, grid, outs, scratch, mib, args, out_specs=None):
    return pl.pallas_call(
        body, grid=(grid,), name=body.__name__,
        in_specs=[pl.BlockSpec(memory_space=pltpu.SMEM) if a.ndim == 1 else VMEM for a in args],
        out_specs=[VMEM] * len(outs) if out_specs is None else out_specs, out_shape=outs,
        scratch_shapes=[pltpu.VMEM(*a) for a in scratch],
        compiler_params=pltpu.CompilerParams(vmem_limit_bytes=mib << 20),
    )(*args)


def stages(n):
    out, rest = [], n
    while rest > 2:
        step = rest // 4 if rest >= 8 else rest // 2
        out.append(tuple(range(step, rest, step)))
        rest = step
    return out


def swap(x, offset, n):
    return lax.ppermute(x, "branch", [(i, i ^ offset) for i in range(n)])


def on_device(queries, branch_keys, branch_values, prefix_keys, prefix_values, cotangent, branch_len):
    n = lax.axis_size("branch")
    slots, width = queries.shape
    heads = width // DH
    plan = stages(n)

    blank = jnp.array(-jnp.inf, BF)
    lo = jnp.maximum(lax.pad(prefix_keys, blank, ((0, 0, 0), (0, DH, 0))),
                     lax.pad(prefix_values, blank, ((0, 0, 0), (DH, 0, 0))))
    turned, rows = sds((heads, DH, slots), BF), sds((slots, DH), BF)
    staged = pl.pallas_call(
        bring, in_specs=[pl.BlockSpec(memory_space=pltpu.HBM)] * 4, out_specs=[VMEM] * 6, name="bring",
        out_shape=[turned, turned, rows, rows, sds((DH, slots), BF), sds((DH, slots), BF)],
        scratch_shapes=[pltpu.VMEM((slots, width), BF), pltpu.VMEM((slots, width), BF), pltpu.SemaphoreType.DMA((4,))],
        compiler_params=pltpu.CompilerParams(vmem_limit_bytes=8 << 20),
    )(queries, cotangent, branch_keys, branch_values)
    for at, offsets in enumerate(plan[:-1]):
        parts = [lo] + [swap(lo, o, n) for o in offsets]
        if at == 0:
            parts, staged = lax.optimization_barrier((parts, staged))
        lo = jnp.concatenate(parts, axis=0)
    qt, gt, kb, vb, kbt, vbt = staged
    parts = [swap(lo, o, n) for o in plan[-1]]
    lows, stat = sds((heads, slots, slots), BF), sds((heads, 8, slots), F32)
    first = call(
        first_forward, heads,
        [lows, sds((heads, lo.shape[0], slots), BF), sds((heads, DH, slots), F32), stat, stat],
        [((DH, lo.shape[0]), BF)], 16, (qt, kb, vbt, lo))
    parts, first = lax.optimization_barrier((parts, first))
    hi = jnp.concatenate(parts, axis=0)
    far = swap(jnp.concatenate([lo, hi], axis=0), 1, n)
    po, p_lo, o, m, l = first

    back = pl.BlockSpec((slots, DH), lambda h: (0, jnp.maximum(h - 1, 0)))
    p_hi, p_far = (sds((heads, a.shape[0], slots), BF) for a in (hi, far))
    att, p_hi, p_far, gs, go, dg, do = call(
        rest_forward, heads + 1,
        [sds((slots, width), BF), p_hi, p_far, turned, turned, stat, stat],
        [((2, hi.shape[0], slots), F32), ((2, far.shape[0], slots), F32), ((2, 8, slots), F32),
         ((DH, hi.shape[0]), BF), ((DH, far.shape[0]), BF)], 24,
        (branch_len, qt, gt, hi, far, o, m, l), [back] + [VMEM] * 6)

    def rows_gradient(p, kv):
        return call(rows_backward, heads, [sds(kv.shape, BF), sds(p.shape, BF)],
                    [((2, kv.shape[0], DH), F32)], 16, (qt, gs, dg, p, kv))

    d_far, ds_far = rows_gradient(p_far, far)
    got = swap(d_far, 1, n)
    d_hi, ds_hi = rows_gradient(p_hi, hi)
    got, d_hi = lax.optimization_barrier((got, d_hi))
    kept = lo.shape[0]
    total = d_hi.astype(F32) + got[kept:].astype(F32)
    parts = [swap(total[kept * i:kept * (i + 1)].astype(BF), o, n) for i, o in enumerate(plan[-1])]
    d_lo, ds_lo, dso, gkb, gvb = call(
        first_backward, heads,
        [sds(lo.shape, BF), sds(p_lo.shape, BF), lows, rows, rows],
        [((2, kept, DH), F32), ((2, slots, DH), F32)], 16,
        (qt, go, do, po, p_lo, kb, vb, lo))
    parts, d_lo = lax.optimization_barrier((parts, d_lo))
    total = d_lo.astype(F32) + got[:kept].astype(F32)
    for part in parts:
        total = total + part.astype(F32)

    gq, = call(
        query_gradient, heads, [sds((slots, width), BF)],
        [((DH, a.shape[0]), BF) for a in (lo, hi, far)], 8,
        (kbt, lo, hi, far, dso, ds_lo, ds_hi, ds_far), [pl.BlockSpec((slots, DH), lambda h: (0, h))])
    for at, offsets in enumerate(reversed(plan[:-1])):
        size = total.shape[0] // (len(offsets) + 1)
        parts = [swap(total[size * (i + 1):size * (i + 2)].astype(BF), o, n) for i, o in enumerate(offsets)]
        total = total[:size]
        if at == 0:
            parts, gq = lax.optimization_barrier((parts, gq))
        for part in parts:
            total = total + part.astype(F32)
    return att, gq, gkb, gvb, total[:, :DH], total[:, DH:]


def solution(mesh):
    row = P(("parts", "branch"), None)
    return jax.shard_map(
        on_device, mesh=mesh, in_specs=(row,) * 6 + (P(("parts", "branch")),), out_specs=(row,) * 6, check_vma=False)
```

```python
import functools
import math

import jax
import jax.numpy as jnp
from jax import lax
from jax.experimental import pallas as pl
from jax.experimental.pallas import tpu as pltpu
from jax.sharding import PartitionSpec as P

DH = 128
FACTOR = DH ** -0.5
SCALE = FACTOR * math.log2(math.e)
F32, BF = jnp.float32, jnp.bfloat16
sds = jax.ShapeDtypeStruct
VMEM = pl.BlockSpec(memory_space=pltpu.VMEM)
OWN = 256


def nn(a, b):
    return lax.dot_general(a, b, (((1,), (0,)), ((), ())), preferred_element_type=F32)


def nt(a, b):
    return lax.dot_general(a, b, (((1,), (1,)), ((), ())), preferred_element_type=F32)


def fold(x, op):
    return op(x.reshape(x.shape[0] // 8, 8, x.shape[1]), axis=0)


def steps(slots):
    own = min(OWN, slots)
    return [(u, u + own) for u in range(0, slots, own)]


def bring(q_any, g_any, kb_any, vb_any, qt_ref, gt_ref, kb_ref, vb_ref, kbt_ref, vbt_ref, q_ref, g_ref, sems):
    pairs = ((q_any, q_ref), (kb_any, kb_ref), (vb_any, vb_ref), (g_any, g_ref))
    copies = [pltpu.make_async_copy(a, b, sems.at[i]) for i, (a, b) in enumerate(pairs)]
    for c in copies:
        c.start()
    for c, a, b in ((copies[0], q_ref, qt_ref), (copies[1], kb_ref, kbt_ref),
                    (copies[2], vb_ref, vbt_ref), (copies[3], g_ref, gt_ref)):
        c.wait()
        if len(b.shape) == 2:
            b[...] = a[...].T
        else:
            for h in range(b.shape[0]):
                b[h] = a[:, h * DH:(h + 1) * DH].T


def summarize(h, slots, pieces, o_ref, m_ref, l_ref):
    top = None
    for s, u, _, _ in pieces:
        t = fold(s, jnp.max)
        if top is not None:
            t = jnp.maximum(top[:, u:], t)
        top = jnp.concatenate([top[:, :u], t], 1) if u else t
    m = top.max(0, keepdims=True) * SCALE
    tot = out = None
    for s, u, vt, put in pieces:
        p = jnp.exp2(s * SCALE - m[:, u:])
        low = p.astype(BF)
        put(low)
        t, o = fold(p, jnp.sum), nn(vt, low)
        if tot is not None:
            t, o = tot[:, u:] + t, out[:, u:] + o
        tot = jnp.concatenate([tot[:, :u], t], 1) if u else t
        out = jnp.concatenate([out[:, :u], o], 1) if u else o
    o_ref[h] = out
    m_ref[h] = jnp.broadcast_to(m, (8, slots))
    l_ref[h] = jnp.broadcast_to(tot.sum(0, keepdims=True), (8, slots))


def own_forward(q_ref, kb_ref, vbt_ref, p_ref, o_ref, m_ref, l_ref):
    h = pl.program_id(0)
    slots = q_ref.shape[2]
    qt = q_ref[h]
    pieces = []
    for u, v in steps(slots):
        s = nn(kb_ref[u:v, :], qt[:, u:])
        ok = lax.broadcasted_iota(jnp.int32, s.shape, 0) <= lax.broadcasted_iota(jnp.int32, s.shape, 1)

        def put(low, u=u, v=v):
            p_ref[h, u:v, u:] = low
        pieces.append((jnp.where(ok, s, -jnp.inf), u, vbt_ref[:, u:v], put))
    summarize(h, slots, pieces, o_ref, m_ref, l_ref)


def block_forward(q_ref, kv_ref, p_ref, o_ref, m_ref, l_ref, vt_ref):
    h = pl.program_id(0)

    @pl.when(h == 0)
    def _():
        vt_ref[...] = kv_ref[:, DH:].T

    def put(low):
        p_ref[h] = low
    summarize(h, q_ref.shape[2], [(nn(kv_ref[:, :DH], q_ref[h]), 0, vt_ref[...], put)], o_ref, m_ref, l_ref)


def rest_forward(len_ref, q_ref, g_ref, hi_ref, far_ref, *refs):
    groups = [refs[3 * i:3 * i + 3] for i in range(3)]
    att_ref, ph_ref, pf_ref = refs[9:12]
    scaled = [refs[12 + 2 * i:14 + 2 * i] for i in range(4)]
    sh_ref, sf_ref, top_ref, vht_ref, vft_ref = refs[20:]
    k = pl.program_id(0)
    heads = pl.num_programs(0) - 1
    slots = q_ref.shape[2]
    now, last = k % 2, (k + 1) % 2
    halves = ((hi_ref, sh_ref, ph_ref, vht_ref), (far_ref, sf_ref, pf_ref, vft_ref))

    def score():
        qt = q_ref[k]
        top = None
        for ref, s_ref, _, _ in halves:
            s = nn(ref[:, :DH], qt)
            s_ref[now] = s
            t = fold(s, jnp.max)
            top = t if top is None else jnp.maximum(top, t)
        top_ref[now] = top

    def finish():
        h = k - 1
        m = top_ref[last].max(0, keepdims=True) * SCALE
        for _, m_ref, _ in groups:
            m = jnp.maximum(m, m_ref[h, :1])
        alphas = [jnp.exp2(m_ref[h, :1] - m) for _, m_ref, _ in groups]
        tot = ot = 0.0
        for alpha, (o_ref, _, l_ref) in zip(alphas, groups):
            tot = tot + alpha * l_ref[h, :1]
            ot = ot + alpha * o_ref[h]
        for _, s_ref, p_ref, vt_ref in halves:
            p = jnp.exp2(s_ref[last] * SCALE - m)
            low = p.astype(BF)
            p_ref[h] = low
            ot = ot + nn(vt_ref[...], low)
            tot = tot + fold(p, jnp.sum).sum(0, keepdims=True)
        live = lax.broadcasted_iota(jnp.int32, (1, slots), 1) < len_ref[0]
        inv = jnp.where(live, 1.0 / tot, 0.0)
        ot = ot * inv
        att_ref[...] = ot.T.astype(BF)
        gt = g_ref[h].astype(F32)
        for scale, (w_ref, d_ref) in zip([inv] + [inv * alpha for alpha in alphas], scaled):
            w = (gt * scale).astype(BF)
            w_ref[h] = w
            d_ref[h] = jnp.broadcast_to((w.astype(F32) * ot).sum(0, keepdims=True), (8, slots))

    @pl.when(k == 0)
    def _():
        vht_ref[...] = hi_ref[:, DH:].T
        vft_ref[...] = far_ref[:, DH:].T
        score()

    @pl.when((k > 0) & (k < heads))
    def _():
        finish()
        score()

    @pl.when(k == heads)
    def _():
        finish()


def gradients(p, kv, ws, dot):
    return p * (nn(kv, ws) - dot).astype(BF)


def rows_backward(q_ref, w_ref, d_ref, p_ref, kv_ref, dkv_ref, ds_ref, acc_ref):
    h = pl.program_id(0)

    @pl.when(h == 0)
    def _():
        acc_ref[...] = jnp.zeros_like(acc_ref)

    ws = w_ref[h]
    p = p_ref[h]
    ds = gradients(p, kv_ref[:, DH:], ws, d_ref[h, :1])
    ds_ref[h] = ds
    acc_ref[1] += nt(p, ws)
    acc_ref[0] += nt(ds, q_ref[h])

    @pl.when(h == pl.num_programs(0) - 1)
    def _():
        dkv_ref[:, :DH] = (acc_ref[0] * FACTOR).astype(BF)
        dkv_ref[:, DH:] = acc_ref[1].astype(BF)


def first_backward(q_ref, wo_ref, do_ref, w_ref, d_ref, po_ref, pl_ref, kb_ref, vb_ref, lo_ref,
                   dkv_ref, dsl_ref, dso_ref, gk_ref, gv_ref, acc_ref, own_ref):
    h = pl.program_id(0)
    slots = q_ref.shape[2]

    @pl.when(h == 0)
    def _():
        acc_ref[...] = jnp.zeros_like(acc_ref)
        own_ref[...] = jnp.zeros_like(own_ref)

    ws, dot, qt = w_ref[h], d_ref[h, :1], q_ref[h]
    p = pl_ref[h]
    ds = gradients(p, lo_ref[:, DH:], ws, dot)
    dsl_ref[h] = ds
    acc_ref[1] += nt(p, ws)
    acc_ref[0] += nt(ds, qt)
    ws, dot = wo_ref[h], do_ref[h, :1]
    for u, v in steps(slots):
        p = po_ref[h, u:v, u:]
        ds = gradients(p, vb_ref[u:v, :], ws[:, u:], dot[:, u:])
        dso_ref[h, u:v, u:] = ds
        own_ref[1, u:v, :] += nt(p, ws[:, u:])
        own_ref[0, u:v, :] += nt(ds, qt[:, u:])

    @pl.when(h == pl.num_programs(0) - 1)
    def _():
        dkv_ref[:, :DH] = (acc_ref[0] * FACTOR).astype(BF)
        dkv_ref[:, DH:] = acc_ref[1].astype(BF)
        gk_ref[...] = (own_ref[0] * FACTOR).astype(BF)
        gv_ref[...] = own_ref[1].astype(BF)


def query_gradient(kbt_ref, ds_ref, *refs):
    count = len(refs) // 3
    gq_ref = refs[2 * count]
    parts = list(zip(refs[:count], refs[count:2 * count], refs[2 * count + 1:]))
    h = pl.program_id(0)
    slots = gq_ref.shape[0]

    @pl.when(h == 0)
    def _():
        for kv_ref, _, kt_ref in parts:
            kt_ref[...] = kv_ref[:, :DH].T

    dq = 0.0
    for _, d_ref, kt_ref in parts:
        dq = dq + nn(kt_ref[...], d_ref[h])
    for u, v in steps(slots):
        o = dq[:, u:] + nn(kbt_ref[:, u:v], ds_ref[h, u:v, u:])
        dq = o if u == 0 else jnp.concatenate([dq[:, :u], o], 1)
    gq_ref[...] = (dq * FACTOR).T.astype(BF)


def call(body, grid, outs, scratch, mib, args, out_specs=None):
    return pl.pallas_call(
        body, grid=(grid,), name=body.__name__,
        in_specs=[pl.BlockSpec(memory_space=pltpu.SMEM) if a.ndim == 1 else VMEM for a in args],
        out_specs=[VMEM] * len(outs) if out_specs is None else out_specs, out_shape=outs,
        scratch_shapes=[pltpu.VMEM(*a) for a in scratch],
        compiler_params=pltpu.CompilerParams(vmem_limit_bytes=mib << 20),
    )(*args)


def stages(n):
    out, rest = [], n
    while rest > 2:
        step = rest // 4 if rest >= 8 else rest // 2
        out.append(tuple(range(step, rest, step)))
        rest = step
    return out


def swap(x, offset, n):
    return lax.ppermute(x, "branch", [(i, i ^ offset) for i in range(n)])


def on_device(queries, branch_keys, branch_values, prefix_keys, prefix_values, cotangent, branch_len):
    n = lax.axis_size("branch")
    slots, width = queries.shape
    heads = width // DH
    plan = stages(n)

    blank = jnp.array(-jnp.inf, BF)
    lo = jnp.maximum(lax.pad(prefix_keys, blank, ((0, 0, 0), (0, DH, 0))),
                     lax.pad(prefix_values, blank, ((0, 0, 0), (DH, 0, 0))))
    turned, rows = sds((heads, DH, slots), BF), sds((slots, DH), BF)
    staged = pl.pallas_call(
        bring, in_specs=[pl.BlockSpec(memory_space=pltpu.HBM)] * 4, out_specs=[VMEM] * 6, name="bring",
        out_shape=[turned, turned, rows, rows, sds((DH, slots), BF), sds((DH, slots), BF)],
        scratch_shapes=[pltpu.VMEM((slots, width), BF), pltpu.VMEM((slots, width), BF), pltpu.SemaphoreType.DMA((4,))],
        compiler_params=pltpu.CompilerParams(vmem_limit_bytes=8 << 20),
    )(*(pltpu.with_memory_space_constraint(a, pltpu.HBM) for a in (queries, cotangent, branch_keys, branch_values)))
    lows, stat, out = sds((heads, slots, slots), BF), sds((heads, 8, slots), F32), sds((heads, DH, slots), F32)
    own = call(own_forward, heads, [lows, out, stat, stat], [], 12, (staged[0], staged[2], staged[5]))
    for at, offsets in enumerate(plan[:-1]):
        parts = [lo] + [swap(lo, o, n) for o in offsets]
        if at == 0:
            parts, staged, own = lax.optimization_barrier((parts, staged, own))
        lo = jnp.concatenate(parts, axis=0)
    qt, gt, kb, vb, kbt, vbt = staged
    kept = lo.shape[0]
    low = sds((heads, kept, slots), BF)

    def forward(kv):
        return call(block_forward, heads, [low, out, stat, stat], [((DH, kept), BF)], 12, (qt, kv))

    parts = [swap(lo, o, n) for o in plan[-1]]
    far_lo = swap(lo, 1, n)
    near = forward(lo)
    far_lo, near = lax.optimization_barrier((far_lo, near))
    far = forward(far_lo)
    parts, near, far = lax.optimization_barrier((parts, near, far))
    hi = jnp.concatenate(parts, axis=0)
    far_hi = swap(hi, 1, n)

    back = pl.BlockSpec((slots, DH), lambda h: (0, jnp.maximum(h - 1, 0)))
    high = sds((heads, hi.shape[0], slots), BF)
    att, p_hi, p_far_hi, *scaled = call(
        rest_forward, heads + 1,
        [sds((slots, width), BF), high, high] + [turned, stat] * 4,
        [((2, hi.shape[0], slots), F32), ((2, hi.shape[0], slots), F32), ((2, 8, slots), F32),
         ((DH, hi.shape[0]), BF), ((DH, hi.shape[0]), BF)], 20,
        (branch_len, qt, gt, hi, far_hi, *own[1:], *near[1:], *far[1:]), [back] + [VMEM] * 10)
    rest_w, own_w, near_w, far_w = (tuple(scaled[2 * i:2 * i + 2]) for i in range(4))

    def backward(w, p, kv):
        return call(rows_backward, heads, [sds(kv.shape, BF), sds(p.shape, BF)],
                    [((2, kv.shape[0], DH), F32)], 12, (qt, *w, p, kv))

    d_far_hi, ds_far_hi = backward(rest_w, p_far_hi, far_hi)
    got = swap(d_far_hi, 1, n)
    d_hi, ds_hi = backward(rest_w, p_hi, hi)
    got, d_hi = lax.optimization_barrier((got, d_hi))
    total = d_hi.astype(F32) + got.astype(F32)
    sends = [total[kept * i:kept * (i + 1)].astype(BF) for i in range(len(plan[-1]))]
    sends, far_w = lax.optimization_barrier((sends, far_w))
    parts = [swap(x, o, n) for x, o in zip(sends, plan[-1])]
    d_far_lo, ds_far_lo = backward(far_w, far[0], far_lo)
    got = swap(d_far_lo, 1, n)
    d_lo, ds_lo, dso, gkb, gvb = call(
        first_backward, heads, [sds(lo.shape, BF), low, lows, rows, rows],
        [((2, kept, DH), F32), ((2, slots, DH), F32)], 16,
        (qt, *own_w, *near_w, own[0], near[0], kb, vb, lo))
    parts, got, d_lo = lax.optimization_barrier((parts, got, d_lo))
    total = d_lo.astype(F32) + got.astype(F32)
    for part in parts:
        total = total + part.astype(F32)

    keys = (lo, far_lo, hi, far_hi)
    gq, = call(
        query_gradient, heads, [sds((slots, width), BF)], [((DH, a.shape[0]), BF) for a in keys], 8,
        (kbt, dso, *keys, ds_lo, ds_far_lo, ds_hi, ds_far_hi), [pl.BlockSpec((slots, DH), lambda h: (0, h))])
    for at, offsets in enumerate(reversed(plan[:-1])):
        size = total.shape[0] // (len(offsets) + 1)
        parts = [swap(total[size * (i + 1):size * (i + 2)].astype(BF), o, n) for i, o in enumerate(offsets)]
        total = total[:size]
        if at == 0:
            parts, gq = lax.optimization_barrier((parts, gq))
        for part in parts:
            total = total + part.astype(F32)
    return att, gq, gkb, gvb, total[:, :DH], total[:, DH:]


def solution(mesh):
    row = P(("parts", "branch"), None)
    return jax.shard_map(
        on_device, mesh=mesh, in_specs=(row,) * 6 + (P(("parts", "branch")),), out_specs=(row,) * 6, check_vma=False)
```

```python
import functools
import math

import jax
import jax.numpy as jnp
from jax import lax
from jax.experimental import pallas as pl
from jax.experimental.pallas import tpu as pltpu
from jax.sharding import PartitionSpec as P

DH = 128
FACTOR = DH ** -0.5
SCALE = FACTOR * math.log2(math.e)
F32, BF = jnp.float32, jnp.bfloat16
sds = jax.ShapeDtypeStruct
VMEM = pl.BlockSpec(memory_space=pltpu.VMEM)
OWN = 256


def nn(a, b):
    return lax.dot_general(a, b, (((1,), (0,)), ((), ())), preferred_element_type=F32)


def nt(a, b):
    return lax.dot_general(a, b, (((1,), (1,)), ((), ())), preferred_element_type=F32)


def fold(x, op):
    return op(x.reshape(x.shape[0] // 8, 8, x.shape[1]), axis=0)


def steps(slots):
    own = min(OWN, slots)
    return [(u, u + own) for u in range(0, slots, own)]


def bring(q_any, g_any, kb_any, vb_any, qt_ref, gt_ref, kb_ref, vb_ref, kbt_ref, vbt_ref, q_ref, g_ref, sems):
    pairs = ((q_any, q_ref), (kb_any, kb_ref), (vb_any, vb_ref), (g_any, g_ref))
    copies = [pltpu.make_async_copy(a, b, sems.at[i]) for i, (a, b) in enumerate(pairs)]
    for c in copies:
        c.start()
    for c, a, b in ((copies[0], q_ref, qt_ref), (copies[1], kb_ref, kbt_ref),
                    (copies[2], vb_ref, vbt_ref), (copies[3], g_ref, gt_ref)):
        c.wait()
        if len(b.shape) == 2:
            b[...] = a[...].T
        else:
            for h in range(b.shape[0]):
                b[h] = a[:, h * DH:(h + 1) * DH].T


def heads_of(ref):
    return range(ref.shape[0])


def chunks(rows, size=512):
    size = math.gcd(rows, size)
    return [slice(c, c + size) for c in range(0, rows, size)]


def join(op, total, x):
    return x if total is None else op(total, x)


def block_scores(q_ref, pieces, h):
    top = None
    for kv_ref, s_ref, *_ in pieces:
        for r in chunks(kv_ref.shape[0]):
            s = nn(kv_ref[r, :DH], q_ref[h])
            s_ref[h % 2, r] = s
            top = join(jnp.maximum, top, fold(s, jnp.max))
    return top


def block_weights(pieces, h, m):
    tot = out = None
    for _, s_ref, p_ref, vt_ref in pieces:
        for r in chunks(s_ref.shape[1], 128):
            p = jnp.exp2(s_ref[h % 2, r] * SCALE - m)
            p_ref[h, r] = p.astype(BF)
            tot = join(jnp.add, tot, fold(p, jnp.sum))
        out = join(jnp.add, out, nn(vt_ref[...], p_ref[h]))
    return tot, out


def own_forward(q_ref, kb_ref, vbt_ref, p_ref, o_ref, m_ref, l_ref, s_ref):
    slots = q_ref.shape[2]

    def score(h):
        top = None
        for u, v in steps(slots):
            s = nn(kb_ref[u:v, :], q_ref[h, :, u:])
            ok = lax.broadcasted_iota(jnp.int32, s.shape, 0) <= lax.broadcasted_iota(jnp.int32, s.shape, 1)
            s = jnp.where(ok, s, -jnp.inf)
            s_ref[h % 2, u:v, u:] = s
            t = fold(s, jnp.max)
            top = jnp.concatenate([top[:, :u], jnp.maximum(top[:, u:], t)], 1) if u else t
        return top

    def weigh(h, m):
        tot = None
        for u, v in steps(slots):
            p = jnp.exp2(s_ref[h % 2, u:v, u:] * SCALE - m[:, u:])
            p_ref[h, u:v, u:] = p.astype(BF)
            t = fold(p, jnp.sum)
            tot = jnp.concatenate([tot[:, :u], tot[:, u:] + t], 1) if u else t
            o = nn(vbt_ref[:, u:v], p_ref[h, u:v, u:])
            if u:
                o_ref[h, :, u:] += o
            else:
                o_ref[h] = o
        return tot

    top = score(0)
    for h in heads_of(q_ref):
        m = top.max(0, keepdims=True) * SCALE
        if h + 1 < q_ref.shape[0]:
            top = score(h + 1)
        tot = weigh(h, m)
        m_ref[h] = jnp.broadcast_to(m, (8, slots))
        l_ref[h] = jnp.broadcast_to(tot.sum(0, keepdims=True), (8, slots))


def block_forward(q_ref, kv_ref, p_ref, o_ref, m_ref, l_ref, vt_ref, s_ref):
    slots = q_ref.shape[2]
    vt_ref[...] = kv_ref[:, DH:].T
    pieces = ((kv_ref, s_ref, p_ref, vt_ref),)
    top = block_scores(q_ref, pieces, 0)
    for h in heads_of(q_ref):
        m = top.max(0, keepdims=True) * SCALE
        if h + 1 < q_ref.shape[0]:
            top = block_scores(q_ref, pieces, h + 1)
        tot, o_ref[h] = block_weights(pieces, h, m)
        m_ref[h] = jnp.broadcast_to(m, (8, slots))
        l_ref[h] = jnp.broadcast_to(tot.sum(0, keepdims=True), (8, slots))


def rest_forward(len_ref, q_ref, g_ref, hi_ref, far_ref, *refs):
    groups = [refs[3 * i:3 * i + 3] for i in range(3)]
    att_ref, ph_ref, pf_ref = refs[9:12]
    scaled = [refs[12 + 2 * i:14 + 2 * i] for i in range(4)]
    sh_ref, sf_ref, vht_ref, vft_ref = refs[20:]
    slots = q_ref.shape[2]
    vht_ref[...] = hi_ref[:, DH:].T
    vft_ref[...] = far_ref[:, DH:].T
    pieces = ((hi_ref, sh_ref, ph_ref, vht_ref), (far_ref, sf_ref, pf_ref, vft_ref))
    live = lax.broadcasted_iota(jnp.int32, (1, slots), 1) < len_ref[0]
    top = block_scores(q_ref, pieces, 0)
    for h in heads_of(q_ref):
        m = top.max(0, keepdims=True) * SCALE
        if h + 1 < q_ref.shape[0]:
            top = block_scores(q_ref, pieces, h + 1)
        for _, m_ref, _ in groups:
            m = jnp.maximum(m, m_ref[h, :1])
        tot, ot = block_weights(pieces, h, m)
        tot = tot.sum(0, keepdims=True)
        alphas = [jnp.exp2(m_ref[h, :1] - m) for _, m_ref, _ in groups]
        for alpha, (o_ref, _, l_ref) in zip(alphas, groups):
            tot = tot + alpha * l_ref[h, :1]
            ot = ot + alpha * o_ref[h]
        inv = jnp.where(live, 1.0 / tot, 0.0)
        ot = ot * inv
        att_ref[:, h * DH:(h + 1) * DH] = ot.T.astype(BF)
        gt = g_ref[h].astype(F32)
        for scale, (w_ref, d_ref) in zip([inv] + [inv * alpha for alpha in alphas], scaled):
            w = (gt * scale).astype(BF)
            w_ref[h] = w
            d_ref[h] = jnp.broadcast_to((w.astype(F32) * ot).sum(0, keepdims=True), (8, slots))


def gradients(p, kv, ws, dot):
    return p * (nn(kv, ws) - dot).astype(BF)


def block_gradient(q_ref, w_ref, d_ref, p_ref, kv_ref, ds_ref, acc_ref, h):
    for r in chunks(kv_ref.shape[0]):
        ds_ref[h, r] = gradients(p_ref[h, r], kv_ref[r, DH:], w_ref[h], d_ref[h, :1])
    dv, dk = nt(p_ref[h], w_ref[h]), nt(ds_ref[h], q_ref[h])
    if h:
        acc_ref[0] += dk
        acc_ref[1] += dv
    else:
        acc_ref[0] = dk
        acc_ref[1] = dv


def rows_backward(q_ref, w_ref, d_ref, p_ref, kv_ref, dkv_ref, ds_ref, acc_ref):
    for h in heads_of(q_ref):
        block_gradient(q_ref, w_ref, d_ref, p_ref, kv_ref, ds_ref, acc_ref, h)
    dkv_ref[:, :DH] = (acc_ref[0] * FACTOR).astype(BF)
    dkv_ref[:, DH:] = acc_ref[1].astype(BF)


def first_backward(q_ref, wo_ref, do_ref, w_ref, d_ref, po_ref, pl_ref, kb_ref, vb_ref, lo_ref,
                   dkv_ref, dsl_ref, dso_ref, gk_ref, gv_ref, acc_ref, own_ref):
    slots = q_ref.shape[2]
    for h in heads_of(q_ref):
        block_gradient(q_ref, w_ref, d_ref, pl_ref, lo_ref, dsl_ref, acc_ref, h)
        for u, v in steps(slots):
            ws, dot = wo_ref[h, :, u:], do_ref[h, :1, u:]
            dso_ref[h, u:v, u:] = gradients(po_ref[h, u:v, u:], vb_ref[u:v, :], ws, dot)
            dv, dk = nt(po_ref[h, u:v, u:], ws), nt(dso_ref[h, u:v, u:], q_ref[h, :, u:])
            if h:
                own_ref[0, u:v, :] += dk
                own_ref[1, u:v, :] += dv
            else:
                own_ref[0, u:v, :] = dk
                own_ref[1, u:v, :] = dv
    dkv_ref[:, :DH] = (acc_ref[0] * FACTOR).astype(BF)
    dkv_ref[:, DH:] = acc_ref[1].astype(BF)
    gk_ref[...] = (own_ref[0] * FACTOR).astype(BF)
    gv_ref[...] = own_ref[1].astype(BF)


def query_gradient(kbt_ref, ds_ref, *refs):
    count = (len(refs) - 4) // 3
    gq_any, kts, (t_ref, gq_ref, sems) = refs[2 * count], refs[2 * count + 1:-3], refs[-3:]
    parts = list(zip(refs[:count], refs[count:2 * count], kts))
    slots = gq_ref.shape[0]
    for kv_ref, _, kt_ref in parts:
        kt_ref[...] = kv_ref[:, :DH].T
    copies = []
    for h in heads_of(ds_ref):
        dq = None
        for _, d_ref, kt_ref in parts:
            dq = join(jnp.add, dq, nn(kt_ref[...], d_ref[h]))
        t_ref[h % 2] = dq
        for u, v in steps(slots):
            t_ref[h % 2, :, u:] += nn(kbt_ref[:, u:v], ds_ref[h, u:v, u:])
        col = slice(h * DH, (h + 1) * DH)
        gq_ref[:, col] = (t_ref[h % 2] * FACTOR).T.astype(BF)
        copies.append(pltpu.make_async_copy(gq_ref.at[:, col], gq_any.at[:, col], sems.at[h]))
        copies[-1].start()
    for c in copies:
        c.wait()


def call(body, outs, scratch, mib, args, out_specs=None):
    return pl.pallas_call(
        body, name=body.__name__,
        in_specs=[pl.BlockSpec(memory_space=pltpu.SMEM) if a.ndim == 1 else VMEM for a in args],
        out_specs=[VMEM] * len(outs) if out_specs is None else out_specs, out_shape=outs,
        scratch_shapes=[pltpu.VMEM(*a) if isinstance(a, tuple) else a for a in scratch],
        compiler_params=pltpu.CompilerParams(vmem_limit_bytes=mib << 20),
    )(*args)


def stages(n):
    out, rest = [], n
    while rest > 2:
        step = rest // 4 if rest >= 8 else rest // 2
        out.append(tuple(range(step, rest, step)))
        rest = step
    return out


def swap(x, offset, n):
    return lax.ppermute(x, "branch", [(i, i ^ offset) for i in range(n)])


def on_device(queries, branch_keys, branch_values, prefix_keys, prefix_values, cotangent, branch_len):
    n = lax.axis_size("branch")
    slots, width = queries.shape
    heads = width // DH
    plan = stages(n)

    blank = jnp.array(-jnp.inf, BF)
    lo = jnp.maximum(lax.pad(prefix_keys, blank, ((0, 0, 0), (0, DH, 0))),
                     lax.pad(prefix_values, blank, ((0, 0, 0), (DH, 0, 0))))
    turned, rows = sds((heads, DH, slots), BF), sds((slots, DH), BF)
    staged = pl.pallas_call(
        bring, in_specs=[pl.BlockSpec(memory_space=pltpu.HBM)] * 4, out_specs=[VMEM] * 6, name="bring",
        out_shape=[turned, turned, rows, rows, sds((DH, slots), BF), sds((DH, slots), BF)],
        scratch_shapes=[pltpu.VMEM((slots, width), BF), pltpu.VMEM((slots, width), BF), pltpu.SemaphoreType.DMA((4,))],
        compiler_params=pltpu.CompilerParams(vmem_limit_bytes=8 << 20),
    )(*(pltpu.with_memory_space_constraint(a, pltpu.HBM) for a in (queries, cotangent, branch_keys, branch_values)))
    lows, stat, out = sds((heads, slots, slots), BF), sds((heads, 8, slots), F32), sds((heads, DH, slots), F32)
    own = call(own_forward, [lows, out, stat, stat], [((2, slots, slots), F32)], 12, (staged[0], staged[2], staged[5]))
    for at, offsets in enumerate(plan[:-1]):
        parts = [lo] + [swap(lo, o, n) for o in offsets]
        if at == 0:
            parts, staged, own = lax.optimization_barrier((parts, staged, own))
        lo = jnp.concatenate(parts, axis=0)
    qt, gt, kb, vb, kbt, vbt = staged
    kept = lo.shape[0]
    low = sds((heads, kept, slots), BF)

    def forward(kv):
        return call(block_forward, [low, out, stat, stat], [((DH, kept), BF), ((2, kept, slots), F32)], 12, (qt, kv))

    parts = [swap(lo, o, n) for o in plan[-1]]
    far_lo = swap(lo, 1, n)
    near = forward(lo)
    far_lo, near = lax.optimization_barrier((far_lo, near))
    far = forward(far_lo)
    parts, near, far = lax.optimization_barrier((parts, near, far))
    hi = jnp.concatenate(parts, axis=0)
    far_hi = swap(hi, 1, n)

    high = sds((heads, hi.shape[0], slots), BF)
    att, p_hi, p_far_hi, *scaled = call(
        rest_forward,
        [sds((slots, width), BF), high, high] + [turned, stat] * 4,
        [((2, hi.shape[0], slots), F32), ((2, hi.shape[0], slots), F32),
         ((DH, hi.shape[0]), BF), ((DH, hi.shape[0]), BF)], 20,
        (branch_len, qt, gt, hi, far_hi, *own[1:], *near[1:], *far[1:]))
    rest_w, own_w, near_w, far_w = (tuple(scaled[2 * i:2 * i + 2]) for i in range(4))

    def backward(w, p, kv):
        return call(rows_backward, [sds(kv.shape, BF), sds(p.shape, BF)],
                    [((2, kv.shape[0], DH), F32)], 12, (qt, *w, p, kv))

    d_far_hi, ds_far_hi = backward(rest_w, p_far_hi, far_hi)
    got = swap(d_far_hi, 1, n)
    d_hi, ds_hi = backward(rest_w, p_hi, hi)
    got, d_hi = lax.optimization_barrier((got, d_hi))
    total = d_hi.astype(F32) + got.astype(F32)
    sends = [total[kept * i:kept * (i + 1)].astype(BF) for i in range(len(plan[-1]))]
    sends, far_w = lax.optimization_barrier((sends, far_w))
    parts = [swap(x, o, n) for x, o in zip(sends, plan[-1])]
    d_far_lo, ds_far_lo = backward(far_w, far[0], far_lo)
    got = swap(d_far_lo, 1, n)
    d_lo, ds_lo, dso, gkb, gvb = call(
        first_backward, [sds(lo.shape, BF), low, lows, rows, rows],
        [((2, kept, DH), F32), ((2, slots, DH), F32)], 16,
        (qt, *own_w, *near_w, own[0], near[0], kb, vb, lo))
    parts, got, d_lo = lax.optimization_barrier((parts, got, d_lo))
    total = d_lo.astype(F32) + got.astype(F32)
    for part in parts:
        total = total + part.astype(F32)

    keys = (lo, far_lo, hi, far_hi)
    gq, = call(
        query_gradient, [sds((slots, width), BF)],
        [((DH, a.shape[0]), BF) for a in keys]
        + [((2, DH, slots), F32), ((slots, width), BF), pltpu.SemaphoreType.DMA((heads,))], 10,
        (kbt, dso, *keys, ds_lo, ds_far_lo, ds_hi, ds_far_hi), [pl.BlockSpec(memory_space=pltpu.HBM)])
    for at, offsets in enumerate(reversed(plan[:-1])):
        size = total.shape[0] // (len(offsets) + 1)
        parts = [swap(total[size * (i + 1):size * (i + 2)].astype(BF), o, n) for i, o in enumerate(offsets)]
        total = total[:size]
        if at == 0:
            parts, gq = lax.optimization_barrier((parts, gq))
        for part in parts:
            total = total + part.astype(F32)
    return att, gq, gkb, gvb, total[:, :DH], total[:, DH:]


def solution(mesh):
    row = P(("parts", "branch"), None)
    return jax.shard_map(
        on_device, mesh=mesh, in_specs=(row,) * 6 + (P(("parts", "branch")),), out_specs=(row,) * 6, check_vma=False)
```

```python
import functools
import math

import jax
import jax.numpy as jnp
from jax import lax
from jax.experimental import pallas as pl
from jax.experimental.pallas import tpu as pltpu
from jax.sharding import PartitionSpec as P


DH = 128
FACTOR = DH ** -0.5
SCALE = FACTOR * math.log2(math.e)
F32, BF = jnp.float32, jnp.bfloat16
sds = jax.ShapeDtypeStruct
VMEM = pl.BlockSpec(memory_space=pltpu.VMEM)
OWN = 256
ONES = 16


def nn(a, b):
    return lax.dot_general(a, b, (((1,), (0,)), ((), ())), preferred_element_type=F32)


def nt(a, b):
    return lax.dot_general(a, b, (((1,), (1,)), ((), ())), preferred_element_type=F32)


def fold(x, op):
    return op(x.reshape(x.shape[0] // 8, 8, x.shape[1]), axis=0)


def steps(slots):
    own = min(OWN, slots)
    return [(u, u + own) for u in range(0, slots, own)]


def bring(q_any, g_any, kb_any, vb_any, qt_ref, gt_ref, kb_ref, vb_ref, kbt_ref, vbt_ref, q_ref, g_ref, sems):
    pairs = ((q_any, q_ref), (kb_any, kb_ref), (vb_any, vb_ref), (g_any, g_ref))
    copies = [pltpu.make_async_copy(a, b, sems.at[i]) for i, (a, b) in enumerate(pairs)]
    for c in copies:
        c.start()
    for c, a, b in ((copies[0], q_ref, qt_ref), (copies[1], kb_ref, kbt_ref),
                    (copies[2], vb_ref, vbt_ref), (copies[3], g_ref, gt_ref)):
        c.wait()
        if len(b.shape) == 2:
            b[...] = a[...].T
        else:
            for h in range(b.shape[0]):
                b[h] = a[:, h * DH:(h + 1) * DH].T


def heads_of(ref):
    return range(ref.shape[0])


def chunks(rows, size=512):
    size = math.gcd(rows, size)
    return [slice(c, c + size) for c in range(0, rows, size)]


def join(op, total, x):
    return x if total is None else op(total, x)


def block_scores(q_ref, pieces, h):
    top = None
    for kv_ref, s_ref, *_ in pieces:
        for r in chunks(kv_ref.shape[0]):
            s = nn(kv_ref[r, :DH], q_ref[h])
            s_ref[h % 2, r] = s
            top = join(jnp.maximum, top, fold(s, jnp.max))
    return top


def block_weights(pieces, h, m):
    out = None
    for _, s_ref, p_ref, vt_ref in pieces:
        for r in chunks(s_ref.shape[1], 128):
            p = jnp.exp2(s_ref[h % 2, r] * SCALE - m)
            p_ref[h, r] = p.astype(BF)
        out = join(jnp.add, out, nn(vt_ref[...], p_ref[h]))
    return out


def turn_values(vt_ref, v):
    vt_ref[:DH] = v.T
    vt_ref[DH:] = jnp.ones((ONES, vt_ref.shape[1]), BF)


def exponent(top):
    return jnp.ceil(top.max(0, keepdims=True) * SCALE)


def ratio(old, new):
    return jnp.exp2(old - new).astype(BF)


def own_forward(q_ref, kb_ref, vbt_ref, p_ref, o_ref, m_ref, l_ref, s_ref):
    slots = q_ref.shape[2]

    def score(h):
        top = None
        for u, v in steps(slots):
            s = nn(kb_ref[u:v, :], q_ref[h, :, u:])
            ok = lax.broadcasted_iota(jnp.int32, s.shape, 0) <= lax.broadcasted_iota(jnp.int32, s.shape, 1)
            s = jnp.where(ok, s, -jnp.inf)
            s_ref[h % 2, u:v, u:] = s
            t = fold(s, jnp.max)
            top = jnp.concatenate([top[:, :u], jnp.maximum(top[:, u:], t)], 1) if u else t
        return top

    def weigh(h, m):
        tot = None
        for u, v in steps(slots):
            p = jnp.exp2(s_ref[h % 2, u:v, u:] * SCALE - m[:, u:])
            low = p.astype(BF)
            p_ref[h, u:v, u:] = low
            t = fold(low.astype(F32), jnp.sum)
            tot = jnp.concatenate([tot[:, :u], tot[:, u:] + t], 1) if u else t
            o = nn(vbt_ref[:, u:v], p_ref[h, u:v, u:])
            if u:
                o_ref[h, :, u:] += o
            else:
                o_ref[h] = o
        return tot

    top = score(0)
    for h in heads_of(q_ref):
        m = exponent(top)
        if h + 1 < q_ref.shape[0]:
            top = score(h + 1)
        tot = weigh(h, m)
        m_ref[h] = jnp.broadcast_to(m, (8, slots))
        l_ref[h] = jnp.broadcast_to(tot.sum(0, keepdims=True), (8, slots))


def block_forward(q_ref, kv_ref, oo_ref, om_ref, ol_ref, p_ref, o_ref, m_ref, l_ref, vt_ref, s_ref):
    slots = q_ref.shape[2]
    turn_values(vt_ref, kv_ref[:, DH:])
    pieces = ((kv_ref, s_ref, p_ref, vt_ref),)
    top = block_scores(q_ref, pieces, 0)
    for h in heads_of(q_ref):
        old = om_ref[h, :1]
        m = jnp.maximum(exponent(top), old)
        if h + 1 < q_ref.shape[0]:
            top = block_scores(q_ref, pieces, h + 1)
        out = block_weights(pieces, h, m)
        alpha = ratio(old, m).astype(F32)
        o_ref[h] = out[:DH] + alpha * oo_ref[h]
        m_ref[h] = jnp.broadcast_to(m, (8, slots))
        l_ref[h] = jnp.broadcast_to(out[DH:DH + 1] + alpha * ol_ref[h, :1], (8, slots))


def score_block(q_ref, k_ref, s_ref, t_ref):
    for h in heads_of(q_ref):
        top = None
        for r in chunks(k_ref.shape[0]):
            s = nn(k_ref[r, :], q_ref[h])
            s_ref[h, r] = s
            top = join(jnp.maximum, top, fold(s, jnp.max))
        t_ref[h] = top


def final_exponent(h, old_ref, *tops):
    m = old_ref[h, :1]
    for t_ref in tops:
        m = jnp.maximum(m, exponent(t_ref[h]))
    return m


def weigh_block(s_ref, v_ref, th_ref, tf_ref, old_ref, p_ref, o_ref, l_ref, vt_ref):
    turn_values(vt_ref, v_ref[...])
    for h in heads_of(s_ref):
        m = final_exponent(h, old_ref, th_ref, tf_ref)
        for r in chunks(s_ref.shape[1], 128):
            p_ref[h, r] = jnp.exp2(s_ref[h, r] * SCALE - m).astype(BF)
        out = nn(vt_ref[...], p_ref[h])
        o_ref[h] = out[:DH]
        l_ref[h] = out[DH:DH + 8]


def rest_forward(len_ref, g_ref, s_ref, v_ref, th_ref, tf_ref, oh_ref, lh_ref, o_ref, l_ref, *refs):
    olds = refs[:3]
    att_ref, p_ref = refs[3:5]
    scaled = [refs[5 + 2 * i:7 + 2 * i] for i in range(4)]
    vt_ref = refs[13]
    slots = g_ref.shape[2]
    turn_values(vt_ref, v_ref[...])
    live = lax.broadcasted_iota(jnp.int32, (1, slots), 1) < len_ref[0]
    for h in heads_of(g_ref):
        m = final_exponent(h, olds[-1], th_ref, tf_ref)
        for r in chunks(s_ref.shape[1], 128):
            p_ref[h, r] = jnp.exp2(s_ref[h, r] * SCALE - m).astype(BF)
        out = nn(vt_ref[...], p_ref[h])
        alphas = [ratio(m_ref[h, :1], m) for m_ref in olds]
        alpha = alphas[-1].astype(F32)
        tot = lh_ref[h, :1] + out[DH:DH + 1] + alpha * l_ref[h, :1]
        inv = jnp.where(live, 1.0 / tot, 0.0)
        ot = (out[:DH] + oh_ref[h] + alpha * o_ref[h]) * inv
        att_ref[:, h * DH:(h + 1) * DH] = ot.T.astype(BF)
        w = (g_ref[h].astype(F32) * inv).astype(BF)
        dot = (w.astype(F32) * ot).sum(0, keepdims=True)
        for alpha, (w_ref, d_ref) in zip([None] + alphas, scaled):
            w_ref[h] = w if alpha is None else w * alpha
            d_ref[h] = jnp.broadcast_to(dot if alpha is None else dot * alpha.astype(F32), (8, slots))


def gradients(p, kv, ws, dot):
    return p * (nn(kv, ws) - dot).astype(BF)


def rows_backward(q_ref, w_ref, d_ref, p_ref, kv_ref, dkv_ref, ds_ref, acc_ref, *, start):
    rows = slice(start, start + dkv_ref.shape[0])
    for h in heads_of(q_ref):
        ds_ref[h] = gradients(p_ref[h, rows], kv_ref[rows, kv_ref.shape[1] - DH:], w_ref[h], d_ref[h, :1])
        dv, dk = nt(p_ref[h, rows], w_ref[h]), nt(ds_ref[h], q_ref[h])
        if h:
            acc_ref[0] += dk
            acc_ref[1] += dv
        else:
            acc_ref[0] = dk
            acc_ref[1] = dv
    dkv_ref[:, :DH] = (acc_ref[0] * FACTOR).astype(BF)
    dkv_ref[:, DH:] = acc_ref[1].astype(BF)


def own_backward(q_ref, w_ref, d_ref, p_ref, kb_ref, vb_ref, ds_ref, gk_ref, gv_ref, acc_ref):
    slots = q_ref.shape[2]
    for h in heads_of(q_ref):
        for u, v in steps(slots):
            ws, dot = w_ref[h, :, u:], d_ref[h, :1, u:]
            ds_ref[h, u:v, u:] = gradients(p_ref[h, u:v, u:], vb_ref[u:v, :], ws, dot)
            dv, dk = nt(p_ref[h, u:v, u:], ws), nt(ds_ref[h, u:v, u:], q_ref[h, :, u:])
            if h:
                acc_ref[0, u:v, :] += dk
                acc_ref[1, u:v, :] += dv
            else:
                acc_ref[0, u:v, :] = dk
                acc_ref[1, u:v, :] = dv
    gk_ref[...] = (acc_ref[0] * FACTOR).astype(BF)
    gv_ref[...] = acc_ref[1].astype(BF)


def query_gradient(kbt_ref, ds_ref, *refs):
    count = (len(refs) - 4) // 3
    gq_any, kts, (t_ref, gq_ref, sems) = refs[2 * count], refs[2 * count + 1:-3], refs[-3:]
    parts = list(zip(refs[:count], refs[count:2 * count], kts))
    slots = gq_ref.shape[0]
    for kv_ref, _, kt_ref in parts:
        kt_ref[...] = kv_ref[:, :DH].T
    copies = []
    for h in heads_of(ds_ref):
        dq = None
        for _, d_ref, kt_ref in parts:
            dq = join(jnp.add, dq, nn(kt_ref[...], d_ref[h]))
        t_ref[h % 2] = dq
        for u, v in steps(slots):
            t_ref[h % 2, :, u:] += nn(kbt_ref[:, u:v], ds_ref[h, u:v, u:])
        col = slice(h * DH, (h + 1) * DH)
        gq_ref[:, col] = (t_ref[h % 2] * FACTOR).T.astype(BF)
        copies.append(pltpu.make_async_copy(gq_ref.at[:, col], gq_any.at[:, col], sems.at[h]))
        copies[-1].start()
    for c in copies:
        c.wait()


def call(body, outs, scratch, mib, args, out_specs=None):
    return pl.pallas_call(
        body,
        in_specs=[pl.BlockSpec(memory_space=pltpu.SMEM) if a.ndim == 1 else VMEM for a in args],
        out_specs=[VMEM] * len(outs) if out_specs is None else out_specs, out_shape=outs,
        scratch_shapes=[pltpu.VMEM(*a) if isinstance(a, tuple) else a for a in scratch],
        compiler_params=pltpu.CompilerParams(vmem_limit_bytes=mib << 20),
    )(*args)


def stages(n):
    out, rest = [], n
    while rest > 2:
        step = rest // 4 if rest >= 8 else rest // 2
        out.append(tuple(range(step, rest, step)))
        rest = step
    return out


def swap(x, offset, n):
    return lax.ppermute(x, "branch", [(i, i ^ offset) for i in range(n)])


def on_device(queries, branch_keys, branch_values, prefix_keys, prefix_values, cotangent, branch_len):
    n = lax.axis_size("branch")
    slots, width = queries.shape
    heads = width // DH
    plan = stages(n)

    blank = jnp.array(-jnp.inf, BF)
    lo = jnp.maximum(lax.pad(prefix_keys, blank, ((0, 0, 0), (0, DH, 0))),
                     lax.pad(prefix_values, blank, ((0, 0, 0), (DH, 0, 0))))
    turned, rows = sds((heads, DH, slots), BF), sds((slots, DH), BF)
    staged = pl.pallas_call(
        bring, in_specs=[pl.BlockSpec(memory_space=pltpu.HBM)] * 4, out_specs=[VMEM] * 6, name="bring",
        out_shape=[turned, turned, rows, rows, sds((DH, slots), BF), sds((DH, slots), BF)],
        scratch_shapes=[pltpu.VMEM((slots, width), BF), pltpu.VMEM((slots, width), BF), pltpu.SemaphoreType.DMA((4,))],
        compiler_params=pltpu.CompilerParams(vmem_limit_bytes=8 << 20),
    )(*(pltpu.with_memory_space_constraint(a, pltpu.HBM) for a in (queries, cotangent, branch_keys, branch_values)))
    lows, stat, out = sds((heads, slots, slots), BF), sds((heads, 8, slots), F32), sds((heads, DH, slots), F32)
    own = call(own_forward, [lows, out, stat, stat], [((2, slots, slots), F32)], 12, (staged[0], staged[2], staged[5]))
    for at, offsets in enumerate(plan[:-1]):
        parts = [lo] + [swap(lo, o, n) for o in offsets]
        if at == 0:
            parts, staged, own = lax.optimization_barrier((parts, staged, own))
        lo = jnp.concatenate(parts, axis=0)
    qt, gt, kb, vb, kbt, _ = staged
    kept = lo.shape[0]
    low = sds((heads, kept, slots), BF)

    def forward(kv, before):
        return call(block_forward, [low, out, stat, stat], [((DH + ONES, kept), BF), ((2, kept, slots), F32)], 12,
                    (qt, kv, *before[1:]))

    parts_k = [swap(lo[:, :DH], o, n) for o in plan[-1]]
    parts_v = [swap(lo[:, DH:], o, n) for o in plan[-1]]
    far_lo = swap(lo, 1, n)
    near = forward(lo, own)
    far_lo, near = lax.optimization_barrier((far_lo, near))
    far = forward(far_lo, near)
    parts_k, near, far = lax.optimization_barrier((parts_k, near, far))
    hi_k = jnp.concatenate(parts_k, axis=0)
    high = sds((heads, hi_k.shape[0], slots), BF)

    def score(k):
        return call(score_block, [sds(high.shape, F32), stat], [], 10, (qt, k))

    far_hi_k = swap(hi_k, 1, n)
    scores = score(hi_k)
    far_hi_k, (s_hi, t_hi) = lax.optimization_barrier((far_hi_k, scores))
    scores = score(far_hi_k)
    parts_v, (s_far, t_far) = lax.optimization_barrier((parts_v, scores))
    hi_v = jnp.concatenate(parts_v, axis=0)
    far_hi_v = swap(hi_v, 1, n)
    turn = [((DH + ONES, hi_v.shape[0]), BF)]
    p_hi, o_hi, l_hi = call(weigh_block, [high, out, stat], turn, 12, (s_hi, hi_v, t_hi, t_far, far[2]))
    far_hi_v, o_hi = lax.optimization_barrier((far_hi_v, o_hi))
    att, p_far_hi, *scaled = call(
        rest_forward, [sds((slots, width), BF), high] + [turned, stat] * 4, turn, 16,
        (branch_len, gt, s_far, far_hi_v, t_hi, t_far, o_hi, l_hi, far[1], far[3], own[2], near[2], far[2]))
    rest_w, own_w, near_w, far_w = (tuple(scaled[2 * i:2 * i + 2]) for i in range(4))

    def backward(w, p, kv, start=0, stop=None):
        count = (kv.shape[0] if stop is None else stop) - start
        return call(functools.partial(rows_backward, start=start), [sds((count, 2 * DH), BF), sds((heads, count, slots), BF)],
                    [((2, count, DH), F32)], 12, (qt, *w, p, kv))

    pieces = [(0, kept * 3 // 4), (kept * 3 // 4, kept)] if len(plan[-1]) == 1 else [(0, hi_v.shape[0])]
    parts, ds_his, ds_fars, w = [], [], [], rest_w
    for a, b in pieces:
        d_far, ds_far = backward(w, p_far_hi, far_hi_v, a, b)
        got = swap(d_far, 1, n)
        d_hi, ds_hi = backward(w, p_hi, hi_v, a, b)
        got, d_hi = lax.optimization_barrier((got, d_hi))
        total = d_hi.astype(F32) + got.astype(F32)
        width_of = total.shape[0] // len(plan[-1])
        sends = [total[width_of * i:width_of * (i + 1)].astype(BF) for i in range(len(plan[-1]))]
        sends, w, far_w, own_w = lax.optimization_barrier((sends, w, far_w, own_w))
        parts.append([swap(x, o, n) for x, o in zip(sends, plan[-1])])
        ds_his.append(ds_hi)
        ds_fars.append(ds_far)
    d_far_lo, ds_far_lo = backward(far_w, far[0], far_lo)
    got = swap(d_far_lo, 1, n)
    d_lo, ds_lo = backward(near_w, near[0], lo)
    parts, got, d_lo, own_w = lax.optimization_barrier((parts, got, d_lo, own_w))
    total = d_lo.astype(F32) + got.astype(F32)
    if len(pieces) > 1:
        parts = [[jnp.concatenate([part[0] for part in parts], axis=0)]]
    for part in parts[0]:
        total = total + part.astype(F32)

    dso, gkb, gvb = call(own_backward, [lows, rows, rows], [((2, slots, DH), F32)], 12, (qt, *own_w, own[0], kb, vb))
    keys = [lo, far_lo] + [hi_k[a:b] for a, b in pieces] + [far_hi_k[a:b] for a, b in pieces]
    gq, = call(
        query_gradient, [sds((slots, width), BF)],
        [((DH, a.shape[0]), BF) for a in keys]
        + [((2, DH, slots), F32), ((slots, width), BF), pltpu.SemaphoreType.DMA((heads,))], 10,
        (kbt, dso, *keys, ds_lo, ds_far_lo, *ds_his, *ds_fars), [pl.BlockSpec(memory_space=pltpu.HBM)])
    for at, offsets in enumerate(reversed(plan[:-1])):
        size = total.shape[0] // (len(offsets) + 1)
        parts = [swap(total[size * (i + 1):size * (i + 2)].astype(BF), o, n) for i, o in enumerate(offsets)]
        total = total[:size]
        if at == 0:
            parts, gq = lax.optimization_barrier((parts, gq))
        for part in parts:
            total = total + part.astype(F32)
    return att, gq, gkb, gvb, total[:, :DH], total[:, DH:]


def solution(mesh):
    row = P(("parts", "branch"), None)

    return jax.shard_map(
        on_device, mesh=mesh, in_specs=(row,) * 6 + (P(("parts", "branch")),), out_specs=(row,) * 6, check_vma=False)
```
